256 devices in a mesh: speech: 16 (over z_hi, y, core), text: 16 (over z_lo, x).
Axes of the slice: x: 4, y: 4, z: 8 (z_hi: 2, z_lo: 4; z = z_hi * 4 + z_lo), core: 2. Of those that a mesh axis runs over, the one named last changes fastest.
Arguments:
- speech_feat: float32 [8192, 512], P('speech', 'text'), may hold values from -4 to 4
- text_feat: float32 [32768, 512], P(('text', 'speech')), may hold values from -4 to 4
- text_pot: float32 [32768], P('text'), may hold values from -1 to 1
- map_grad: float32 [8192, 512], P('speech', 'text'), may hold values from -1024 to 1024
Outputs:
- speech_grad: float32 [8192, 512], P('speech', 'text')
- text_grad: float32 [32768, 512], P(('text', 'speech'))
The draws below stay inside these ranges and needn't reach their ends.
All inputs are finite; a program needn't handle non-finite values.
Results may differ from the reference program's by a relative error of at most 0.0003.
Values sent between devices are 32-bit elements; how exact they have to be, the bound alone decides.
A program may use at most 64 MiB of HBM per device.

```python
import math
import jax
import jax.numpy as jnp
from jax import lax

D = 512
SP_DEV = 512
NS = 8192
NT = 32768


def levels(stream_key, shape, split, least, top_value):
    gain = 1.0
    for dim, parts in split:
        heights = jax.random.uniform(jax.random.fold_in(jax.random.fold_in(stream_key, 6), dim), (parts,), jnp.float32, least / len(split), top_value / len(split))
        gain = gain * jnp.repeat(jnp.exp(heights), shape[dim] // parts).reshape((-1,) + (1,) * (len(shape) - 1 - dim))
    return gain


def bell_draw(rng, shape, spread, limit, split=(), kind=jnp.bfloat16):
    values = spread * jax.random.normal(rng, shape, jnp.float32)
    if split:
        values = values * levels(rng, shape, split, -0.22, 0.18)
    return jnp.clip(values, -limit, limit).astype(kind)


def setup_inputs(seed: int = 0) -> dict:
    key_of = jax.random.split(jax.random.key(seed), 5)
    speech_feat = bell_draw(key_of[0], (NS, D), 1.0, 4.0, ((0, 16), (1, 16)), jnp.float32)
    text_feat = bell_draw(key_of[1], (NT, D), 1.0, 4.0, ((0, 256),), jnp.float32)
    text_pot = jnp.clip(jax.random.uniform(key_of[2], (NT,), jnp.float32, -1.0, 1.0) * levels(key_of[2], (NT,), ((0, 16),), -0.4, 0.0), -1.0, 1.0)
    map_grad = bell_draw(key_of[3], (NS, D), (NT / (2 * NS ** 0.5)), 1024.0, ((0, 16), (1, 16)), jnp.float32)
    return dict(speech_feat=speech_feat, text_feat=text_feat, text_pot=text_pot, map_grad=map_grad)


def reference(speech_feat, text_feat, text_pot, map_grad):
    scale = 1.0 / math.sqrt(D)
    highest = lax.Precision.HIGHEST

    def block_step(text_grad, block_index):
        offset = (block_index * SP_DEV).astype(jnp.int32)
        frames = lax.dynamic_slice_in_dim(speech_feat, offset, SP_DEV)
        grads = lax.dynamic_slice_in_dim(map_grad, offset, SP_DEV)
        feat_dots = jnp.dot(frames, text_feat.T, precision=highest, preferred_element_type=jnp.float32)
        grad_dots = jnp.dot(grads, text_feat.T, precision=highest, preferred_element_type=jnp.float32)
        plan_tile = jnp.exp(text_pot[None, :] + scale * feat_dots)
        mass = lax.optimization_barrier(jnp.sum(plan_tile, axis=1))
        first = jnp.dot(plan_tile, text_feat, precision=highest, preferred_element_type=jnp.float32)
        second = jnp.dot(plan_tile * grad_dots, text_feat, precision=highest, preferred_element_type=jnp.float32)
        dots = lax.optimization_barrier(jnp.sum(grads * first, axis=1)) / mass
        speech_block = scale / mass[:, None] * (second - dots[:, None] * first)
        shared = plan_tile / mass[:, None]
        weighted = shared * (grad_dots - dots[:, None])
        added = jnp.dot(shared.T, grads, precision=highest, preferred_element_type=jnp.float32)
        added = added + scale * jnp.dot(weighted.T, frames, precision=highest, preferred_element_type=jnp.float32)
        return (text_grad + added, speech_block)
    text_grad, blocks = lax.scan(block_step, jnp.zeros((NT, D), jnp.float32), jnp.arange(NS // SP_DEV, dtype=jnp.int32))
    return (blocks.reshape(NS, D), text_grad)
```

```python
import math

import jax
import jax.numpy as jnp
from jax import lax
from jax.experimental import pallas as pl
from jax.experimental.pallas import tpu as pltpu
from jax.sharding import PartitionSpec as P

D = 512
F = 512
T = 2048
TB = 128
SCALE = 1.0 / math.sqrt(D)
BF = jnp.bfloat16
F32 = jnp.float32
MESH = pl.DeviceIdType.MESH

NAMES = (
    ["z1", "z2", "z3"]
    + [f"{k}{r}" for r in range(4) for k in ("xp", "xm", "fp", "fm")]
    + ["za", "zb", "zaf", "zbf"]
    + [f"{k}{q}" for q in range(2) for k in ("yp", "ym", "fyp", "fym", "sb0", "sb1", "sb2", "sb3")]
    + [f"st{k}" for k in range(1, 16)]
    + [f"cs{q}{d}" for q in range(2) for d in range(4)]
    + [f"{k}{q}" for q in range(2) for k in ("ra", "rb", "rc", "rd")]
    + ["wa", "wb", "waf", "wbf"]
    + ["ua", "ub", "uc", "ud", "v1", "v2", "v3"]
)
SEM = {name: k for k, name in enumerate(NAMES)}


def halves(v):
    hi = v.astype(BF)
    return hi, (v - hi.astype(F32)).astype(BF)


def dot(a, b):
    return lax.dot_general(a, b, (((1,), (0,)), ((), ())), preferred_element_type=F32)


def kernel(
    x_ref, g_ref, t_ref, pot_ref, sg_ref, tg_ref,
    xg, tb, xh, xl, tth, ttl, rh, rl, potb, pm, gdm, wh, wl, acc, st,
    cp, sbuf, ys, ry2, ry1, rla, rlb, rla2, rlb2, zr,
    sp, xs, rx2, rx1, rz,
    ssem, rsem, lsem,
):
    s_me = lax.axis_index("speech")
    t_me = lax.axis_index("text")
    zh, y, c = s_me // 8, (s_me // 2) % 4, s_me % 2
    zl, x = t_me // 4, t_me % 4
    z = zh * 4 + zl

    def dev(zh_, y_, c_, zl_, x_):
        return {"speech": (zh_ * 4 + y_) * 2 + c_, "text": zl_ * 4 + x_}

    def at_z(zz):
        return dev(zz // 4, y, c, zz % 4, x)

    yp_, ym_ = (y + 1) % 4, (y + 3) % 4
    xp_, xm_ = (x + 1) % 4, (x + 3) % 4
    sib = dev(zh, y, 1 - c, zl, x)
    up_y, dn_y = dev(zh, yp_, c, zl, x), dev(zh, ym_, c, zl, x)
    up_x, dn_x = dev(zh, y, c, zl, xp_), dev(zh, y, c, zl, xm_)
    up_z, dn_z = at_z((z + 2) % 8), at_z((z + 6) % 8)
    pending = []

    def copy(name, src, dst, to):
        k = SEM[name]
        return pltpu.make_async_remote_copy(
            src_ref=src, dst_ref=dst, send_sem=ssem.at[k], recv_sem=rsem.at[k], device_id=to, device_id_type=MESH
        )

    def send(name, src, dst, to):
        one = copy(name, src, dst, to)
        one.start()
        pending.append(one)

    def got(name, ref):
        copy(name, ref, ref, sib).wait_recv()

    def xg_at(zl_, x_, lo=0, n=32):
        return xg.at[pl.ds(pl.multiple_of((zl_ * 4 + x_) * 32 + lo, 16), n), :]

    def tb_at(zh_, y_, c_, lo=0, n=TB):
        return tb.at[pl.ds(pl.multiple_of(((zh_ * 4 + y_) * 2 + c_) * TB + lo, 64), n), :]

    own_rows = pl.ds(pl.multiple_of(t_me * 32, 32), 32)
    local = [
        pltpu.make_async_copy(x_ref, xg.at[own_rows, pl.ds(0, F)], lsem.at[0]),
        pltpu.make_async_copy(g_ref, xg.at[own_rows, pl.ds(F, F)], lsem.at[1]),
        pltpu.make_async_copy(t_ref, tb_at(zh, y, c), lsem.at[2]),
    ]
    for one in local:
        one.start()
    barrier = pltpu.get_barrier_semaphore()
    text_peers = []
    for k in range(1, 16):
        to = {"speech": s_me, "text": (t_me + k) % 16}
        text_peers.append(to)
        pl.semaphore_signal(barrier, inc=1, device_id=to, device_id_type=MESH)
    for to in (sib, up_y, dn_y, up_z, dn_z):
        pl.semaphore_signal(barrier, inc=1, device_id=to, device_id_type=MESH)
    for one in local:
        one.wait()
    pl.semaphore_wait(barrier, 20)

    def z_send(r):
        send(f"z{r}", xg_at(zl, x), xg_at(zl, x), dev(zh, y, c, (zl + r) % 4, x))

    def x_send(r):
        zs = (zl + 4 - r) % 4
        send(f"xp{r}", xg_at(zs, x), xg_at(zs, x), up_x)
        send(f"xm{r}", xg_at(zs, x), xg_at(zs, x), dn_x)

    def x_forward(r):
        zs = (zl + 4 - r) % 4
        got(f"xp{r}", xg_at(zs, xm_))
        send(f"fp{r}", xg_at(zs, xm_, 0, 16), xg_at(zs, xm_, 0, 16), up_x)
        got(f"xm{r}", xg_at(zs, xp_))
        send(f"fm{r}", xg_at(zs, xp_, 16, 16), xg_at(zs, xp_, 16, 16), dn_x)

    def x_last(r):
        zs, x2 = (zl + 4 - r) % 4, (x + 2) % 4
        got(f"fp{r}", xg_at(zs, x2, 0, 16))
        got(f"fm{r}", xg_at(zs, x2, 16, 16))

    def zq_of(q):
        return zh if q == 0 else 1 - zh

    def y_send(q):
        zq = zq_of(q)
        send(f"yp{q}", tb_at(zq, y, c), tb_at(zq, y, c), up_y)
        send(f"ym{q}", tb_at(zq, y, c), tb_at(zq, y, c), dn_y)
        send(f"sb0{q}", tb_at(zq, y, c), tb_at(zq, y, c), sib)

    def y_forward(q):
        zq = zq_of(q)
        got(f"yp{q}", tb_at(zq, ym_, c))
        send(f"fyp{q}", tb_at(zq, ym_, c, 0, 64), tb_at(zq, ym_, c, 0, 64), up_y)
        send(f"sb1{q}", tb_at(zq, ym_, c), tb_at(zq, ym_, c), sib)
        got(f"ym{q}", tb_at(zq, yp_, c))
        send(f"fym{q}", tb_at(zq, yp_, c, 64, 64), tb_at(zq, yp_, c, 64, 64), dn_y)
        send(f"sb2{q}", tb_at(zq, yp_, c), tb_at(zq, yp_, c), sib)

    def y_last(q):
        zq, y2 = zq_of(q), (y + 2) % 4
        got(f"fyp{q}", tb_at(zq, y2, c, 0, 64))
        got(f"fym{q}", tb_at(zq, y2, c, 64, 64))
        send(f"sb3{q}", tb_at(zq, y2, c), tb_at(zq, y2, c), sib)

    def sib_got(q, k):
        zq = zq_of(q)
        got(f"sb{k}{q}", tb_at(zq, (y, ym_, yp_, (y + 2) % 4)[k], 1 - c))

    for r in (1, 2, 3):
        z_send(r)
    x_send(0)
    send("za", tb_at(zh, y, c, 0, 64), rla, up_z)
    send("zb", tb_at(zh, y, c, 64, 64), rlb, dn_z)
    y_send(0)

    def pot_step(k, _):
        row = jnp.broadcast_to(pot_ref[pl.ds(k, 1), :], (128, 128))
        potb[pl.ds(pl.multiple_of(k * 128, 128), 128), :] = jnp.transpose(row)
        return 0

    lax.fori_loop(0, 16, pot_step, 0)

    got("z1", xg_at((zl + 3) % 4, x))
    x_send(1)
    x_forward(0)
    zo_dn, zo_up = (z + 6) % 8, (z + 2) % 8
    got("za", rla)
    send("zaf", rla, tb_at(zo_dn // 4, y, c, 0, 64), up_z)
    got("zb", rlb)
    send("zbf", rlb, tb_at(zo_up // 4, y, c, 64, 64), dn_z)
    got("z2", xg_at((zl + 2) % 4, x))
    x_send(2)
    got("z3", xg_at((zl + 1) % 4, x))
    x_send(3)
    y_forward(0)
    x_forward(1)
    got("zaf", tb_at(1 - zh, y, c, 0, 64))
    got("zbf", tb_at(1 - zh, y, c, 64, 64))
    y_send(1)

    def prep_rows(r0):
        tt = jnp.transpose(tb[pl.ds(r0, 256), :])
        hi, lo = halves(tt)
        tth[:, pl.ds(r0, 256)] = hi
        ttl[:, pl.ds(r0, 256)] = lo

    def row0(zq, yy):
        return pl.multiple_of((zq * 4 + yy) * 256, 256)

    x_forward(2)
    x_forward(3)
    y_last(0)
    for k in range(4):
        sib_got(0, k)

    def prep0(k, _):
        prep_rows(row0(zh, k))
        return 0

    lax.fori_loop(0, 4, prep0, 0)
    y_forward(1)
    for r in range(4):
        x_last(r)

    def split_x(k, _):
        rows = pl.ds(pl.multiple_of(k * 64, 64), 64)
        hi, lo = halves(xg[rows, :])
        xh[rows, :] = hi
        xl[rows, :] = lo
        return 0

    lax.fori_loop(0, 8, split_x, 0)

    acc[...] = jnp.zeros_like(acc)

    def plan_rows(r0):
        rows = pl.ds(r0, 256)
        hi, lo = halves(tb[rows, :])
        prod = dot(
            jnp.concatenate([hi, lo, hi], axis=1),
            jnp.concatenate([xh[...], xh[...], xl[...]], axis=0),
        )
        pot = potb[rows, :]
        p = jnp.exp(prod[:, :F] * SCALE + jnp.concatenate([pot] * 4, axis=1))
        gd = prod[:, F:]
        pm[rows, :] = p
        gdm[rows, :] = gd
        acc[0:8, :] += jnp.sum(p.reshape(32, 8, F), axis=0)
        acc[8:16, :] += jnp.sum((p * gd).reshape(32, 8, F), axis=0)

    def plan0(k, _):
        plan_rows(row0(zh, k))
        return 0

    lax.fori_loop(0, 4, plan0, 0)
    y_last(1)
    for k in range(4):
        sib_got(1, k)

    def plan1(k, _):
        plan_rows(row0(1 - zh, k))
        return 0

    lax.fori_loop(0, 4, plan1, 0)

    mine = st.at[t_me]
    mass_part = jnp.sum(acc[0:8, :], axis=0, keepdims=True)
    dots_part = jnp.sum(acc[8:16, :], axis=0, keepdims=True)
    for k in range(4):
        mine[k : k + 1, :] = mass_part[:, k * 128 : (k + 1) * 128]
        mine[k + 4 : k + 5, :] = dots_part[:, k * 128 : (k + 1) * 128]
    for k in range(1, 16):
        send(f"st{k}", mine, mine, text_peers[k - 1])

    def prep1(k, _):
        prep_rows(row0(1 - zh, k))
        return 0

    lax.fori_loop(0, 4, prep1, 0)

    def right_x(k, _):
        cols = pl.ds(pl.multiple_of(k * 128, 128), 128)
        hi, lo = halves(jnp.transpose(xg[:, cols]) * SCALE)
        rows = pl.ds(pl.multiple_of(F + k * 128, 128), 128)
        rh[rows, :] = hi
        rl[rows, :] = lo
        return 0

    def right_g(k, _):
        cols = pl.ds(pl.multiple_of(F + k * 128, 128), 128)
        hi, lo = halves(jnp.transpose(xg[:, cols]))
        rows = pl.ds(pl.multiple_of(k * 128, 128), 128)
        rh[rows, :] = hi
        rl[rows, :] = lo
        return 0

    lax.fori_loop(0, 4, right_x, 0)
    lax.fori_loop(0, 4, right_g, 0)

    for k in range(1, 16):
        got(f"st{k}", st.at[(t_me + 16 - k) % 16])
    total = jnp.sum(st[...], axis=0)
    mass = jnp.concatenate([total[k : k + 1, :] for k in range(4)], axis=1)
    inv = 1.0 / mass
    dots = jnp.concatenate([total[k : k + 1, :] for k in range(4, 8)], axis=1) / mass

    def text_block(q, d):
        zq = zq_of(q)
        yd = (y + d) % 4
        rows = pl.ds(row0(zq, yd), 256)
        sh = pm[rows, :] * inv
        w = sh * (gdm[rows, :] - dots)
        sh_hi, sh_lo = halves(sh)
        w_hi, w_lo = halves(w)
        wh[rows, :] = w_hi
        wl[rows, :] = w_lo
        out = dot(
            jnp.concatenate([sh_hi, w_hi, sh_lo, w_lo, sh_hi, w_hi], axis=1),
            jnp.concatenate([rh[...], rh[...], rl[...]], axis=0),
        )
        cp[zq, yd] = out.reshape(2, TB, D)

    def cross(q, d):
        zq, yd = zq_of(q), (y + d) % 4
        send(f"cs{q}{d}", cp.at[zq, yd, 1 - c], sbuf.at[q, d], sib)

    def text_pair(q, first):
        def step(k, _):
            text_block(q, 2 - k if first else 3 - 3 * k)
            return 0

        lax.fori_loop(0, 2, step, 0)
        for d in (2, 1) if first else (3, 0):
            cross(q, d)

    def chip_sum(q, d):
        got(f"cs{q}{d}", sbuf.at[q, d])
        return cp[zq_of(q), (y + d) % 4, c] + sbuf[q, d]

    def far_y(q):
        ys[q, 2] = chip_sum(q, 2)
        send(f"ra{q}", ys.at[q, 2, pl.ds(0, 64)], ry2.at[q, 0], up_y)
        send(f"rb{q}", ys.at[q, 2, pl.ds(64, 64)], ry2.at[q, 1], dn_y)

    def near_y(q):
        one = chip_sum(q, 1)
        got(f"ra{q}", ry2.at[q, 0])
        ys[q, 1, 0:64] = one[0:64] + ry2[q, 0]
        ys[q, 1, 64:128] = one[64:128]
        send(f"rc{q}", ys.at[q, 1], ry1.at[q, 0], up_y)
        two = chip_sum(q, 3)
        got(f"rb{q}", ry2.at[q, 1])
        ys[q, 3, 0:64] = two[0:64]
        ys[q, 3, 64:128] = two[64:128] + ry2[q, 1]
        send(f"rd{q}", ys.at[q, 3], ry1.at[q, 1], dn_y)

    def own_y(q):
        one = chip_sum(q, 0)
        got(f"rc{q}", ry1.at[q, 0])
        got(f"rd{q}", ry1.at[q, 1])
        ys[q, 0] = one + (ry1[q, 0] + ry1[q, 1])

    text_pair(1, True)
    far_y(1)
    text_pair(1, False)
    near_y(1)
    text_pair(0, True)
    far_y(0)
    text_pair(0, False)

    def speech_rows(m, _):
        rows = pl.ds(pl.multiple_of(m * 256, 256), 256)
        hi, lo = tth[rows, :], ttl[rows, :]
        out = dot(
            jnp.concatenate([hi, lo, hi], axis=1),
            jnp.concatenate([wh[...], wh[...], wl[...]], axis=0),
        )
        sp[pl.ds(m * 2, 2)] = out.reshape(2, 4, 32, F)
        return 0

    near_y(0)
    own_y(1)
    send("wa", ys.at[1, 0, pl.ds(0, 64)], rla2, up_z)
    send("wb", ys.at[1, 0, pl.ds(64, 64)], rlb2, dn_z)
    lax.fori_loop(0, 2, speech_rows, 0)
    x2 = (x + 2) % 4
    send("ua", sp.at[:, x2, pl.ds(0, 16)], rx2.at[0], up_x)
    send("ub", sp.at[:, x2, pl.ds(16, 16)], rx2.at[1], dn_x)
    got("wa", rla2)
    send("waf", rla2, zr.at[pl.ds(0, 64)], up_z)
    got("wb", rlb2)
    send("wbf", rlb2, zr.at[pl.ds(64, 64)], dn_z)
    got("ua", rx2.at[0])
    xs[0, :, 0:16] = sp[:, xp_, 0:16] + rx2[0]
    xs[0, :, 16:32] = sp[:, xp_, 16:32]
    send("uc", xs.at[0], rx1.at[0], up_x)
    got("ub", rx2.at[1])
    xs[1, :, 0:16] = sp[:, xm_, 0:16]
    xs[1, :, 16:32] = sp[:, xm_, 16:32] + rx2[1]
    send("ud", xs.at[1], rx1.at[1], dn_x)
    got("uc", rx1.at[0])
    got("ud", rx1.at[1])
    xs[2] = sp[:, x] + (rx1[0] + rx1[1])
    for r in (1, 2, 3):
        zt = (zl + r) % 4
        send(f"v{r}", xs.at[2, zt], rz.at[r - 1], dev(zh, y, c, zt, x))
    own_y(0)
    for r in (1, 2, 3):
        got(f"v{r}", rz.at[r - 1])
    sg_ref[...] = (xs[2, zl] + (rz[0] + (rz[1] + rz[2]))) * SCALE
    got("waf", zr.at[pl.ds(0, 64)])
    got("wbf", zr.at[pl.ds(64, 64)])
    tg_ref[...] = ys[0, 0] + zr[...]
    for one in pending:
        one.wait_send()


def solution(mesh):
    def v(shape, kind=F32):
        return pltpu.VMEM(shape, kind)

    scratch = [
        v((D, 2 * F)), v((T, D)), v((D, 2 * F), BF), v((D, 2 * F), BF),
        v((D, T), BF), v((D, T), BF), v((2 * F, D), BF), v((2 * F, D), BF),
        v((T, 128)), v((T, F)), v((T, F)), v((T, F), BF), v((T, F), BF), v((16, F)), v((16, 8, 128)),
        v((2, 4, 2, TB, D)), v((2, 4, TB, D)), v((2, 4, TB, D)), v((2, 2, 64, D)), v((2, 2, TB, D)),
        v((64, D)), v((64, D)), v((64, D)), v((64, D)), v((TB, D)),
        v((4, 4, 32, F)), v((3, 4, 32, F)), v((2, 4, 16, F)), v((2, 4, 32, F)), v((3, 32, F)),
        pltpu.SemaphoreType.DMA((len(NAMES),)),
        pltpu.SemaphoreType.DMA((len(NAMES),)),
        pltpu.SemaphoreType.DMA((3,)),
    ]
    anywhere = pl.BlockSpec(memory_space=pl.ANY)
    vmem = pl.BlockSpec(memory_space=pltpu.VMEM)
    call = pl.pallas_call(
        kernel,
        out_shape=(jax.ShapeDtypeStruct((32, F), F32), jax.ShapeDtypeStruct((TB, D), F32)),
        in_specs=[anywhere, anywhere, anywhere, vmem],
        out_specs=(vmem, vmem),
        scratch_shapes=scratch,
        compiler_params=pltpu.CompilerParams(
            collective_id=0, has_side_effects=True, vmem_limit_bytes=62 * 1024 * 1024
        ),
    )

    def shards(speech_feat, text_feat, text_pot, map_grad):
        sg, tg = call(speech_feat.T, map_grad.T, text_feat, text_pot.reshape(16, 128))
        return sg.T, tg

    return jax.shard_map(
        shards,
        mesh=mesh,
        in_specs=(P("speech", "text"), P(("text", "speech"), None), P("text"), P("speech", "text")),
        out_specs=(P("speech", "text"), P(("text", "speech"), None)),
        check_vma=False,
    )
```

```python
import math

import jax
import jax.numpy as jnp
from jax import lax
from jax.experimental import pallas as pl
from jax.experimental.pallas import tpu as pltpu
from jax.sharding import PartitionSpec as P

D = 512
F = 512
T = 2048
TB = 128
SCALE = 1.0 / math.sqrt(D)
BF = jnp.bfloat16
F32 = jnp.float32
MESH = pl.DeviceIdType.MESH

NAMES = (
    [f"{k}{j}" for j in (1, 2, 3) for k in ("zu", "zd")]
    + [f"{k}{r}" for r in range(4) for k in ("xp", "xm", "fp", "fm")]
    + [f"{k}{h}{p}" for h in (1, 2, 3, 4) for p in range(2) for k in ("tu", "td")]
    + [f"{k}{q}" for q in range(3) for k in ("yp", "ym", "fyp", "fym", "sb0", "sb1", "sb2", "sb3")]
    + [f"st{k}" for k in range(1, 16)]
    + [f"cs{q}{d}" for q in range(2) for d in range(4)]
    + [f"{k}{q}{p}" for q in range(2) for p in range(2) for k in ("ra", "rb", "rc", "rd", "re", "rf")]
    + [f"w{p}" for p in range(2)]
    + [f"{k}{m}" for m in range(2) for k in ("ua", "ub", "uc", "ud", "ue", "uf")]
    + ["v1", "v2", "v3"]
)
SEM = {name: k for k, name in enumerate(NAMES)}


def halves(v):
    hi = v.astype(BF)
    return hi, (v - hi.astype(F32)).astype(BF)


def dot(a, b):
    return lax.dot_general(a, b, (((1,), (0,)), ((), ())), preferred_element_type=F32)


def kernel(
    x_ref, g_ref, t_ref, pot_ref, sg_ref, tg_ref,
    xg, tb, xh, xl, tth, ttl, rh, rl, potb, pm, gdm, wh, wl, acc, st,
    cp, sbuf, ys, ry2, ry1, zr, ru, rd,
    sp, xs, xo, rx2, rx1, rz,
    ssem, rsem, lsem,
):
    s_me = lax.axis_index("speech")
    t_me = lax.axis_index("text")
    zh, y, c = s_me // 8, (s_me // 2) % 4, s_me % 2
    zl, x = t_me // 4, t_me % 4
    z = zh * 4 + zl

    def dev(zh_, y_, c_, zl_, x_):
        return {"speech": (zh_ * 4 + y_) * 2 + c_, "text": zl_ * 4 + x_}

    def at_z(zz):
        return dev(zz // 4, y, c, zz % 4, x)

    yp_, ym_ = (y + 1) % 4, (y + 3) % 4
    xp_, xm_ = (x + 1) % 4, (x + 3) % 4
    sib = dev(zh, y, 1 - c, zl, x)
    up_y, dn_y = dev(zh, yp_, c, zl, x), dev(zh, ym_, c, zl, x)
    up_x, dn_x = dev(zh, y, c, zl, xp_), dev(zh, y, c, zl, xm_)
    far_z = at_z((z + 4) % 8)
    up_z, dn_z = at_z((z + 1) % 8), at_z((z + 7) % 8)
    pending = []

    def copy(name, src, dst, to):
        k = SEM[name]
        return pltpu.make_async_remote_copy(
            src_ref=src, dst_ref=dst, send_sem=ssem.at[k], recv_sem=rsem.at[k], device_id=to, device_id_type=MESH
        )

    def send(name, src, dst, to, track=True):
        one = copy(name, src, dst, to)
        one.start()
        if track:
            pending.append(one)

    def got(name, ref):
        copy(name, ref, ref, sib).wait_recv()

    def xg_at(zl_, x_, lo=0, n=32):
        return xg.at[pl.ds(pl.multiple_of((zl_ * 4 + x_) * 32 + lo, 16), n), :]

    def tb_at(zh_, y_, c_, lo=0, n=TB):
        return tb.at[zh_, y_, c_, pl.ds(lo, n), :]

    own_rows = pl.ds(pl.multiple_of(t_me * 32, 32), 32)
    local = [
        pltpu.make_async_copy(x_ref, xg.at[own_rows, pl.ds(0, F)], lsem.at[0]),
        pltpu.make_async_copy(g_ref, xg.at[own_rows, pl.ds(F, F)], lsem.at[1]),
        pltpu.make_async_copy(t_ref, tb_at(zh, y, c), lsem.at[2]),
    ]
    for one in local:
        one.start()
    barrier = pltpu.get_barrier_semaphore()
    text_peers = []
    for k in range(1, 16):
        to = {"speech": s_me, "text": (t_me + k) % 16}
        text_peers.append(to)
        pl.semaphore_signal(barrier, inc=1, device_id=to, device_id_type=MESH)
    for to in (sib, up_y, dn_y, far_z, up_z, dn_z):
        pl.semaphore_signal(barrier, inc=1, device_id=to, device_id_type=MESH)
    for one in local:
        one.wait()
    pl.semaphore_wait(barrier, 21)

    def line_up(j):
        block = xg_at(zl + 1 - j, x)
        return (zl <= 2) & (zl >= j - 1), copy(f"zu{j}", block, block, dev(zh, y, c, zl + 1, x))

    def line_down(j):
        block = xg_at(zl + j - 1, x)
        return (zl >= 1) & (zl <= 4 - j), copy(f"zd{j}", block, block, dev(zh, y, c, zl - 1, x))

    def line_send(j):
        for fits, one in (line_up(j), line_down(j)):

            @pl.when(fits)
            def _(one=one):
                one.start()

    def line_got(j):
        @pl.when(zl >= j)
        def _():
            got(f"zu{j}", xg_at(zl - j, x))

        @pl.when(zl <= 3 - j)
        def _():
            got(f"zd{j}", xg_at(zl + j, x))

    def line_step(j):
        line_got(j)
        if j < 3:
            line_send(j + 1)
        by_step(j, x_send)

    def by_step(j, do):
        if j == 2:
            do(2)
            return
        for r, here in ((1, zl >= 1), (3, zl <= 2)) if j == 1 else ((3, zl == 3), (1, zl == 0)):

            @pl.when(here)
            def _(r=r):
                do(r, False)

    def x_send(r, track=True):
        zs = (zl + 4 - r) % 4
        send(f"xp{r}", xg_at(zs, x), xg_at(zs, x), up_x, track)
        send(f"xm{r}", xg_at(zs, x), xg_at(zs, x), dn_x, track)

    def x_forward(r, track=True):
        zs = (zl + 4 - r) % 4
        got(f"xp{r}", xg_at(zs, xm_))
        send(f"fp{r}", xg_at(zs, xm_, 0, 16), xg_at(zs, xm_, 0, 16), up_x, track)
        got(f"xm{r}", xg_at(zs, xp_))
        send(f"fm{r}", xg_at(zs, xp_, 16, 16), xg_at(zs, xp_, 16, 16), dn_x, track)

    def x_sent(r):
        zs = (zl + 4 - r) % 4
        for name, lo, n in (("xp", 0, 32), ("xm", 0, 32), ("fp", 0, 16), ("fm", 16, 16)):
            pending.append(copy(f"{name}{r}", xg_at(zs, x, lo, n), xg_at(zs, x, lo, n), up_x))

    def x_last(r):
        zs, x2 = (zl + 4 - r) % 4, (x + 2) % 4
        got(f"fp{r}", xg_at(zs, x2, 0, 16))
        got(f"fm{r}", xg_at(zs, x2, 16, 16))

    def zq_of(q):
        return zh if q == 0 else 1 - zh

    def parcel(g):
        return (zh, 0, TB) if g == 0 else (1 - zh, (g - 1) * 64, 64)

    def y_send(g):
        zq, lo, n = parcel(g)
        send(f"yp{g}", tb_at(zq, y, c, lo, n), tb_at(zq, y, c, lo, n), up_y)
        send(f"ym{g}", tb_at(zq, y, c, lo, n), tb_at(zq, y, c, lo, n), dn_y)
        send(f"sb0{g}", tb_at(zq, y, c, lo, n), tb_at(zq, y, c, lo, n), sib)

    def y_forward(g):
        zq, lo, n = parcel(g)
        h = n // 2
        got(f"yp{g}", tb_at(zq, ym_, c, lo, n))
        send(f"fyp{g}", tb_at(zq, ym_, c, lo, h), tb_at(zq, ym_, c, lo, h), up_y)
        got(f"ym{g}", tb_at(zq, yp_, c, lo, n))
        send(f"fym{g}", tb_at(zq, yp_, c, lo + h, h), tb_at(zq, yp_, c, lo + h, h), dn_y)
        send(f"sb1{g}", tb_at(zq, ym_, c, lo, n), tb_at(zq, ym_, c, lo, n), sib)
        send(f"sb2{g}", tb_at(zq, yp_, c, lo, n), tb_at(zq, yp_, c, lo, n), sib)

    def y_last(g):
        zq, lo, n = parcel(g)
        h, y2 = n // 2, (y + 2) % 4
        got(f"fyp{g}", tb_at(zq, y2, c, lo, h))
        got(f"fym{g}", tb_at(zq, y2, c, lo + h, h))
        send(f"sb3{g}", tb_at(zq, y2, c, lo, n), tb_at(zq, y2, c, lo, n), sib)

    def sib_got(g, ks=(0, 1, 2, 3)):
        zq, lo, n = parcel(g)
        for k in ks:
            got(f"sb{k}{g}", tb_at(zq, (y, ym_, yp_, (y + 2) % 4)[k], 1 - c, lo, n))

    def t_hop(h):
        for p in range(2):
            u, d = pl.ds(64 * p, 32), pl.ds(64 * p + 32, 32)
            if h == 1:
                src_u, src_d = tb.at[zh, y, c, u], tb.at[zh, y, c, d]
            else:
                src_u, src_d = ru.at[h - 2, p], rd.at[h - 2, p]
                got(f"tu{h - 1}{p}", src_u)
                got(f"td{h - 1}{p}", src_d)
            if h == 4:
                dst_u, dst_d = tb.at[((z + 5) % 8) // 4, y, c, u], tb.at[((z + 3) % 8) // 4, y, c, d]
            else:
                dst_u, dst_d = ru.at[h - 1, p], rd.at[h - 1, p]
            send(f"tu{h}{p}", src_u, dst_u, up_z)
            send(f"td{h}{p}", src_d, dst_d, dn_z)

    def z_arrived(p):
        got(f"tu4{p}", tb_at(1 - zh, y, c, 64 * p, 32))
        got(f"td4{p}", tb_at(1 - zh, y, c, 64 * p + 32, 32))
        y_send(p + 1)

    line_send(1)
    x_send(0)
    t_hop(1)
    y_send(0)

    def pot_step(k, _):
        row = jnp.broadcast_to(pot_ref[pl.ds(k, 1), :], (128, 128))
        potb[k] = jnp.transpose(row)
        return 0

    lax.fori_loop(0, 16, pot_step, 0)

    def prep_rows(zq, yy):
        hi, lo = halves(jnp.transpose(tb[zq, yy].reshape(256, D)))
        cols = pl.ds(pl.multiple_of((zq * 4 + yy) * 256, 256), 256)
        tth[:, cols] = hi
        ttl[:, cols] = lo

    def split_x(k, _):
        rows = pl.ds(pl.multiple_of(k * 64, 64), 64)
        hi, lo = halves(xg[rows, :])
        xh[rows, :] = hi
        xl[rows, :] = lo
        return 0

    def plan_part(rows_t, pot, put):
        hi, lo = halves(rows_t)
        prod = dot(
            jnp.concatenate([hi, lo, hi], axis=1),
            jnp.concatenate([xh[...], xh[...], xl[...]], axis=0),
        )
        p = jnp.exp(prod[:, :F] * SCALE + jnp.concatenate([pot] * 4, axis=1))
        gd = prod[:, F:]
        put(p, gd)
        acc[0:8, :] += jnp.sum(p.reshape(32, 8, F), axis=0)
        acc[8:16, :] += jnp.sum((p * gd).reshape(32, 8, F), axis=0)

    def plan_block(zq, yy):
        def put(p, gd):
            pm[zq, yy] = p.reshape(2, TB, F)
            gdm[zq, yy] = gd.reshape(2, TB, F)

        pot = potb[pl.ds((zq * 4 + yy) * 2, 2)].reshape(256, 128)
        plan_part(tb[zq, yy].reshape(256, D), pot, put)

    def plan_piece(zq, two_y, p):
        rows = pl.ds(64 * p, 64)

        def put(p_, gd):
            for k, yy in enumerate(two_y):
                part = slice(128 * k, 128 * k + 128)
                pm[zq, yy, :, rows, :] = p_[part].reshape(2, 64, F)
                gdm[zq, yy, :, rows, :] = gd[part].reshape(2, 64, F)

        pot = jnp.concatenate([potb[pl.ds((zq * 4 + yy) * 2, 2), rows, :].reshape(128, 128) for yy in two_y], axis=0)
        tok = jnp.concatenate([tb[zq, yy, :, rows, :].reshape(128, D) for yy in two_y], axis=0)
        plan_part(tok, pot, put)

    def loop(n, step):
        lax.fori_loop(0, n, lambda k, _: (step(k), 0)[1], 0)

    acc[...] = jnp.zeros_like(acc)
    line_step(1)
    x_forward(0)
    t_hop(2)
    y_forward(0)
    line_step(2)
    by_step(1, x_forward)
    t_hop(3)
    y_last(0)
    line_step(3)
    by_step(2, x_forward)
    sib_got(0)
    t_hop(4)
    by_step(3, x_forward)
    loop(4, lambda k: prep_rows(zh, k))
    z_arrived(0)
    z_arrived(1)
    for r in range(4):
        x_last(r)
    for r in (1, 3):
        x_sent(r)
    lax.fori_loop(0, 8, split_x, 0)
    plan_block(zh, 0)
    y_forward(1)
    plan_block(zh, 1)
    y_forward(2)
    loop(2, lambda k: plan_block(zh, k + 2))
    sib_got(1, (0, 1))
    plan_piece(1 - zh, (y, ym_), 0)
    y_last(1)
    sib_got(2, (0, 1))
    plan_piece(1 - zh, (y, ym_), 1)
    y_last(2)
    sib_got(1, (2, 3))
    plan_piece(1 - zh, (yp_, (y + 2) % 4), 0)
    sib_got(2, (2, 3))
    plan_piece(1 - zh, (yp_, (y + 2) % 4), 1)

    mine = st.at[t_me]
    mass_part = jnp.sum(acc[0:8, :], axis=0, keepdims=True)
    dots_part = jnp.sum(acc[8:16, :], axis=0, keepdims=True)
    for k in range(4):
        mine[k : k + 1, :] = mass_part[:, k * 128 : (k + 1) * 128]
        mine[k + 4 : k + 5, :] = dots_part[:, k * 128 : (k + 1) * 128]
    for k in range(1, 16):
        send(f"st{k}", mine, mine, text_peers[k - 1])

    loop(4, lambda k: prep_rows(1 - zh, k))

    def right_x(k, _):
        cols = pl.ds(pl.multiple_of(k * 128, 128), 128)
        hi, lo = halves(jnp.transpose(xg[:, cols]) * SCALE)
        rows = pl.ds(pl.multiple_of(F + k * 128, 128), 128)
        rh[rows, :] = hi
        rl[rows, :] = lo
        return 0

    def right_g(k, _):
        cols = pl.ds(pl.multiple_of(F + k * 128, 128), 128)
        hi, lo = halves(jnp.transpose(xg[:, cols]))
        rows = pl.ds(pl.multiple_of(k * 128, 128), 128)
        rh[rows, :] = hi
        rl[rows, :] = lo
        return 0

    lax.fori_loop(0, 4, right_x, 0)
    lax.fori_loop(0, 4, right_g, 0)

    for k in range(1, 16):
        got(f"st{k}", st.at[(t_me + 16 - k) % 16])
    total = jnp.sum(st[...], axis=0)
    mass = jnp.concatenate([total[k : k + 1, :] for k in range(4)], axis=1)
    inv = 1.0 / mass
    dots = jnp.concatenate([total[k : k + 1, :] for k in range(4, 8)], axis=1) / mass

    def rows_of(q, d):
        zq, yd = zq_of(q), (y + d) % 4
        return zq, yd, pl.ds(pl.multiple_of((zq * 4 + yd) * 256, 256), 256)

    def weigh(q, d):
        zq, yd, rows = rows_of(q, d)
        sh = pm[zq, yd].reshape(256, F) * inv
        w_hi, w_lo = halves(sh * (gdm[zq, yd].reshape(256, F) - dots))
        wh[rows, :] = w_hi
        wl[rows, :] = w_lo
        return sh, w_hi, w_lo

    def text_block(q, d):
        zq, yd, rows = rows_of(q, d)
        if q == 1:
            sh, w_hi, w_lo = weigh(q, d)
        else:
            sh, w_hi, w_lo = pm[zq, yd].reshape(256, F) * inv, wh[rows, :], wl[rows, :]
        sh_hi, sh_lo = halves(sh)
        out = dot(
            jnp.concatenate([sh_hi, w_hi, sh_lo, w_lo, sh_hi, w_hi], axis=1),
            jnp.concatenate([rh[...], rh[...], rl[...]], axis=0),
        )
        cp[zq, yd] = out.reshape(2, TB, D)
        send(f"cs{q}{d}", cp.at[zq, yd, 1 - c], sbuf.at[q, d], sib)

    def chip_sum(q, d):
        got(f"cs{q}{d}", sbuf.at[q, d])
        return cp[zq_of(q), (y + d) % 4, c] + sbuf[q, d]

    def upper(p):
        return pl.ds(64 * p, 32)

    def lower(p):
        return pl.ds(64 * p + 32, 32)

    def far_y(q):
        ys[q, 2] = chip_sum(q, 2)
        for p in range(2):
            send(f"ra{q}{p}", ys.at[q, 2, upper(p)], ry2.at[q, p, 0], up_y)
            send(f"rb{q}{p}", ys.at[q, 2, lower(p)], ry2.at[q, p, 1], dn_y)

    def near_sums(q):
        ys[q, 1] = chip_sum(q, 1)
        ys[q, 3] = chip_sum(q, 3)

    def free_y(q, p):
        send(f"re{q}{p}", ys.at[q, 1, lower(p)], ry1.at[q, 0, lower(p)], up_y)
        send(f"rf{q}{p}", ys.at[q, 3, upper(p)], ry1.at[q, 1, upper(p)], dn_y)

    def near_y(q, p):
        got(f"ra{q}{p}", ry2.at[q, p, 0])
        ys[q, 1, upper(p)] += ry2[q, p, 0]
        send(f"rc{q}{p}", ys.at[q, 1, upper(p)], ry1.at[q, 0, upper(p)], up_y)
        got(f"rb{q}{p}", ry2.at[q, p, 1])
        ys[q, 3, lower(p)] += ry2[q, p, 1]
        send(f"rd{q}{p}", ys.at[q, 3, lower(p)], ry1.at[q, 1, lower(p)], dn_y)

    def own_y(q, p):
        got(f"re{q}{p}", ry1.at[q, 0, lower(p)])
        got(f"rf{q}{p}", ry1.at[q, 1, upper(p)])
        got(f"rc{q}{p}", ry1.at[q, 0, upper(p)])
        got(f"rd{q}{p}", ry1.at[q, 1, lower(p)])
        rows = pl.ds(64 * p, 64)
        ys[q, 0, rows] += ry1[q, 0, rows] + ry1[q, 1, rows]

    def own_z(p):
        own_y(1, p)
        rows = pl.ds(64 * p, 64)
        send(f"w{p}", ys.at[1, 0, rows], zr.at[rows], far_z)

    def speech_rows(m):
        rows = pl.ds(m * 256, 256)
        hi, lo = tth[rows, :], ttl[rows, :]
        out = dot(
            jnp.concatenate([hi, lo, hi], axis=1),
            jnp.concatenate([wh[...], wh[...], wl[...]], axis=0),
        )
        sp[pl.ds(m * 2, 2)] = out.reshape(2, 4, 32, F)

    x2 = (x + 2) % 4
    top, low = pl.ds(0, 16), pl.ds(16, 16)

    def far_x(m):
        two = pl.ds(2 * m, 2)
        send(f"ua{m}", sp.at[two, x2, top], rx2.at[0, two], up_x)
        send(f"ub{m}", sp.at[two, x2, low], rx2.at[1, two], dn_x)
        send(f"ue{m}", sp.at[two, xp_, low], rx1.at[0, two, low], up_x)
        send(f"uf{m}", sp.at[two, xm_, top], rx1.at[1, two, top], dn_x)

    def near_x(m):
        two = pl.ds(2 * m, 2)
        got(f"ua{m}", rx2.at[0, two])
        xs[0, two] = sp[two, xp_, 0:16] + rx2[0, two]
        send(f"uc{m}", xs.at[0, two], rx1.at[0, two, top], up_x)
        got(f"ub{m}", rx2.at[1, two])
        xs[1, two] = sp[two, xm_, 16:32] + rx2[1, two]
        send(f"ud{m}", xs.at[1, two], rx1.at[1, two, low], dn_x)

    def own_x(m):
        two = pl.ds(2 * m, 2)
        got(f"ue{m}", rx1.at[0, two, low])
        got(f"uf{m}", rx1.at[1, two, top])
        got(f"uc{m}", rx1.at[0, two, top])
        got(f"ud{m}", rx1.at[1, two, low])
        xo[two] = sp[two, x] + (rx1[0, two] + rx1[1, two])

    text_block(1, 2)
    text_block(1, 1)
    far_y(1)
    text_block(1, 3)
    text_block(1, 0)
    near_sums(1)
    free_y(1, 0)
    loop(4, lambda k: weigh(0, k))
    speech_rows(0)
    near_y(1, 0)
    free_y(1, 1)
    far_x(0)
    near_y(1, 1)
    ys[1, 0] = chip_sum(1, 0)
    speech_rows(1)
    far_x(1)
    text_block(0, 2)
    own_z(0)
    text_block(0, 1)
    far_y(0)
    own_z(1)
    near_x(0)
    text_block(0, 3)
    near_x(1)
    text_block(0, 0)
    near_sums(0)
    free_y(0, 0)
    free_y(0, 1)
    near_y(0, 0)
    near_y(0, 1)
    ys[0, 0] = chip_sum(0, 0)
    own_x(0)
    own_x(1)
    for r in (1, 2, 3):
        zt = (zl + r) % 4
        send(f"v{r}", xo.at[zt], rz.at[r - 1], dev(zh, y, c, zt, x))
    own_y(0, 0)
    own_y(0, 1)
    for p in range(2):
        got(f"w{p}", zr.at[pl.ds(64 * p, 64)])
    tg_ref[...] = ys[0, 0] + zr[...]
    for r in (1, 2, 3):
        got(f"v{r}", rz.at[r - 1])
    sg_ref[...] = (xo[zl] + (rz[0] + (rz[1] + rz[2]))) * SCALE
    for j in (1, 2, 3):
        for fits, one in (line_up(j), line_down(j)):

            @pl.when(fits)
            def _(one=one):
                one.wait_send()

    for one in pending:
        one.wait_send()


def finish(sg_ref, tg_ref, sg_out, tg_out):
    sg_out[...] = sg_ref[...]
    tg_out[...] = tg_ref[...]


def solution(mesh):
    def v(shape, kind=F32):
        return pltpu.VMEM(shape, kind)

    scratch = [
        v((D, 2 * F)), v((2, 4, 2, TB, D)), v((D, 2 * F), BF), v((D, 2 * F), BF),
        v((D, T), BF), v((D, T), BF), v((2 * F, D), BF), v((2 * F, D), BF),
        v((16, TB, 128)), v((2, 4, 2, TB, F)), v((2, 4, 2, TB, F)), v((T, F), BF), v((T, F), BF), v((16, F)), v((16, 8, 128)),
        v((2, 4, 2, TB, D)), v((2, 4, TB, D)), v((2, 4, TB, D)), v((2, 2, 2, 32, D)), v((2, 2, TB, D)),
        v((TB, D)), v((3, 2, 32, D)), v((3, 2, 32, D)),
        v((4, 4, 32, F)), v((2, 4, 16, F)), v((4, 32, F)), v((2, 4, 16, F)), v((2, 4, 32, F)), v((3, 32, F)),
        pltpu.SemaphoreType.DMA((len(NAMES),)),
        pltpu.SemaphoreType.DMA((len(NAMES),)),
        pltpu.SemaphoreType.DMA((3,)),
    ]
    anywhere = pl.BlockSpec(memory_space=pl.ANY)
    vmem = pl.BlockSpec(memory_space=pltpu.VMEM)
    call = pl.pallas_call(
        kernel,
        out_shape=(jax.ShapeDtypeStruct((32, F), F32), jax.ShapeDtypeStruct((TB, D), F32)),
        in_specs=[anywhere, anywhere, anywhere, vmem],
        out_specs=(vmem, vmem),
        scratch_shapes=scratch,
        compiler_params=pltpu.CompilerParams(
            collective_id=0, has_side_effects=True, vmem_limit_bytes=62 * 1024 * 1024
        ),
    )

    last = pl.pallas_call(
        finish,
        out_shape=(jax.ShapeDtypeStruct((32, F), F32), jax.ShapeDtypeStruct((TB, D), F32)),
        in_specs=[vmem, vmem],
        out_specs=(vmem, vmem),
    )

    def shards(speech_feat, text_feat, text_pot, map_grad):
        sg, tg = last(*call(speech_feat.T, map_grad.T, text_feat, text_pot.reshape(16, 128)))
        return sg.T, tg

    return jax.shard_map(
        shards,
        mesh=mesh,
        in_specs=(P("speech", "text"), P(("text", "speech"), None), P("text"), P("speech", "text")),
        out_specs=(P("speech", "text"), P(("text", "speech"), None)),
        check_vma=False,
    )
```

```python
import math

import jax
import jax.numpy as jnp
from jax import lax
from jax.experimental import pallas as pl
from jax.experimental.pallas import tpu as pltpu
from jax.sharding import PartitionSpec as P

D = 512
F = 512
T = 2048
TB = 128
SCALE = 1.0 / math.sqrt(D)
BF = jnp.bfloat16
F32 = jnp.float32
MESH = pl.DeviceIdType.MESH

NAMES = (
    [f"{k}{j}" for j in (1, 2, 3) for k in ("zu", "zd")]
    + [f"{k}{r}" for r in range(4) for k in ("xp", "xm", "fp", "fm")]
    + [f"{k}{h}{p}" for h in (1, 2, 3, 4) for p in range(2) for k in ("tu", "td")]
    + [f"{k}{q}" for q in range(3) for k in ("yp", "ym", "fyp", "fym", "sb0", "sb1", "sb2", "sb3")]
    + [f"st{k}" for k in range(1, 16)]
    + [f"cs{q}{d}" for q in range(2) for d in range(4)]
    + [f"{k}{p}" for p in range(2) for k in ("ra", "rb", "rc", "rd", "re", "rf")]
    + [f"{k}{p}" for p in range(4) for k in ("qf", "qu", "qd", "w")]
    + [f"{k}{m}" for m in range(2) for k in ("ua", "ub", "uc", "ud", "ue", "uf")]
    + ["v1", "v2", "v3"]
)
SEM = {name: k for k, name in enumerate(NAMES)}


def halves(v):
    hi = v.astype(BF)
    return hi, (v - hi.astype(F32)).astype(BF)


def dot(a, b):
    return lax.dot_general(a, b, (((1,), (0,)), ((), ())), preferred_element_type=F32)


def kernel(
    x_ref, g_ref, t_ref, pot_ref, sg_ref, tg_ref,
    xg, tb, xh, xl, tth, ttl, rh, rl, potb, pm, gdm, wh, wl, acc, st,
    cp, sbuf, ys, ry2, ry1, qfar, zr, ru, rd,
    sp, xs, xo, rx2, rx1, rz,
    ssem, rsem, lsem,
):
    s_me = lax.axis_index("speech")
    t_me = lax.axis_index("text")
    zh, y, c = s_me // 8, (s_me // 2) % 4, s_me % 2
    zl, x = t_me // 4, t_me % 4
    z = zh * 4 + zl

    def dev(zh_, y_, c_, zl_, x_):
        return {"speech": (zh_ * 4 + y_) * 2 + c_, "text": zl_ * 4 + x_}

    def at_z(zz):
        return dev(zz // 4, y, c, zz % 4, x)

    yp_, ym_ = (y + 1) % 4, (y + 3) % 4
    xp_, xm_ = (x + 1) % 4, (x + 3) % 4
    sib = dev(zh, y, 1 - c, zl, x)
    up_y, dn_y = dev(zh, yp_, c, zl, x), dev(zh, ym_, c, zl, x)
    up_x, dn_x = dev(zh, y, c, zl, xp_), dev(zh, y, c, zl, xm_)
    far_z = at_z((z + 4) % 8)
    up_z, dn_z = at_z((z + 1) % 8), at_z((z + 7) % 8)
    pending = []

    def copy(name, src, dst, to):
        k = SEM[name]
        return pltpu.make_async_remote_copy(
            src_ref=src, dst_ref=dst, send_sem=ssem.at[k], recv_sem=rsem.at[k], device_id=to, device_id_type=MESH
        )

    def send(name, src, dst, to, track=True):
        one = copy(name, src, dst, to)
        one.start()
        if track:
            pending.append(one)

    def got(name, ref):
        copy(name, ref, ref, sib).wait_recv()

    def xg_at(zl_, x_, lo=0, n=32):
        return xg.at[pl.ds(pl.multiple_of((zl_ * 4 + x_) * 32 + lo, 16), n), :]

    def tb_at(zh_, y_, c_, lo=0, n=TB):
        return tb.at[zh_, y_, c_, pl.ds(lo, n), :]

    own_rows = pl.ds(pl.multiple_of(t_me * 32, 32), 32)
    local = [
        pltpu.make_async_copy(x_ref, xg.at[own_rows, pl.ds(0, F)], lsem.at[0]),
        pltpu.make_async_copy(g_ref, xg.at[own_rows, pl.ds(F, F)], lsem.at[1]),
        pltpu.make_async_copy(t_ref, tb_at(zh, y, c), lsem.at[2]),
    ]
    for one in local:
        one.start()
    barrier = pltpu.get_barrier_semaphore()
    text_peers = [{"speech": s_me, "text": (t_me + k) % 16} for k in range(1, 16)]
    for to in (sib, up_y, dn_y, up_x, dn_x, up_z, dn_z):
        pl.semaphore_signal(barrier, inc=1, device_id=to, device_id_type=MESH)
    for one in local:
        one.wait()
    pl.semaphore_wait(barrier, 7)

    def line_up(j):
        block = xg_at(zl + 1 - j, x)
        return (zl <= 2) & (zl >= j - 1), copy(f"zu{j}", block, block, dev(zh, y, c, zl + 1, x))

    def line_down(j):
        block = xg_at(zl + j - 1, x)
        return (zl >= 1) & (zl <= 4 - j), copy(f"zd{j}", block, block, dev(zh, y, c, zl - 1, x))

    def line_send(j):
        for fits, one in (line_up(j), line_down(j)):

            @pl.when(fits)
            def _(one=one):
                one.start()

    def line_got(j):
        @pl.when(zl >= j)
        def _():
            got(f"zu{j}", xg_at(zl - j, x))

        @pl.when(zl <= 3 - j)
        def _():
            got(f"zd{j}", xg_at(zl + j, x))

    def line_step(j):
        line_got(j)
        if j < 3:
            line_send(j + 1)
        by_step(j, x_send)

    def by_step(j, do):
        if j == 2:
            do(2)
            return
        for r, here in ((1, zl >= 1), (3, zl <= 2)) if j == 1 else ((3, zl == 3), (1, zl == 0)):

            @pl.when(here)
            def _(r=r):
                do(r, False)

    def x_send(r, track=True):
        zs = (zl + 4 - r) % 4
        send(f"xp{r}", xg_at(zs, x), xg_at(zs, x), up_x, track)
        send(f"xm{r}", xg_at(zs, x), xg_at(zs, x), dn_x, track)

    def x_forward(r, track=True):
        zs = (zl + 4 - r) % 4
        got(f"xp{r}", xg_at(zs, xm_))
        send(f"fp{r}", xg_at(zs, xm_, 0, 16), xg_at(zs, xm_, 0, 16), up_x, track)
        got(f"xm{r}", xg_at(zs, xp_))
        send(f"fm{r}", xg_at(zs, xp_, 16, 16), xg_at(zs, xp_, 16, 16), dn_x, track)

    def x_sent(r):
        zs = (zl + 4 - r) % 4
        for name, lo, n in (("xp", 0, 32), ("xm", 0, 32), ("fp", 0, 16), ("fm", 16, 16)):
            pending.append(copy(f"{name}{r}", xg_at(zs, x, lo, n), xg_at(zs, x, lo, n), up_x))

    def x_last(r):
        zs, x2 = (zl + 4 - r) % 4, (x + 2) % 4
        got(f"fp{r}", xg_at(zs, x2, 0, 16))
        got(f"fm{r}", xg_at(zs, x2, 16, 16))

    def zq_of(q):
        return zh if q == 0 else 1 - zh

    def parcel(g):
        return (zh, 0, TB) if g == 0 else (1 - zh, (g - 1) * 64, 64)

    def y_send(g):
        zq, lo, n = parcel(g)
        send(f"yp{g}", tb_at(zq, y, c, lo, n), tb_at(zq, y, c, lo, n), up_y)
        send(f"ym{g}", tb_at(zq, y, c, lo, n), tb_at(zq, y, c, lo, n), dn_y)
        send(f"sb0{g}", tb_at(zq, y, c, lo, n), tb_at(zq, y, c, lo, n), sib)

    def y_forward(g):
        zq, lo, n = parcel(g)
        h = n // 2
        got(f"yp{g}", tb_at(zq, ym_, c, lo, n))
        send(f"fyp{g}", tb_at(zq, ym_, c, lo, h), tb_at(zq, ym_, c, lo, h), up_y)
        got(f"ym{g}", tb_at(zq, yp_, c, lo, n))
        send(f"fym{g}", tb_at(zq, yp_, c, lo + h, h), tb_at(zq, yp_, c, lo + h, h), dn_y)
        send(f"sb1{g}", tb_at(zq, ym_, c, lo, n), tb_at(zq, ym_, c, lo, n), sib)
        send(f"sb2{g}", tb_at(zq, yp_, c, lo, n), tb_at(zq, yp_, c, lo, n), sib)

    def y_last(g):
        zq, lo, n = parcel(g)
        h, y2 = n // 2, (y + 2) % 4
        got(f"fyp{g}", tb_at(zq, y2, c, lo, h))
        got(f"fym{g}", tb_at(zq, y2, c, lo + h, h))
        send(f"sb3{g}", tb_at(zq, y2, c, lo, n), tb_at(zq, y2, c, lo, n), sib)

    def sib_got(g, ks=(0, 1, 2, 3)):
        zq, lo, n = parcel(g)
        for k in ks:
            got(f"sb{k}{g}", tb_at(zq, (y, ym_, yp_, (y + 2) % 4)[k], 1 - c, lo, n))

    def t_hop(h):
        for p in range(2):
            u, d = pl.ds(64 * p, 32), pl.ds(64 * p + 32, 32)
            if h == 1:
                src_u, src_d = tb.at[zh, y, c, u], tb.at[zh, y, c, d]
            else:
                src_u, src_d = ru.at[h - 2, p], rd.at[h - 2, p]
                got(f"tu{h - 1}{p}", src_u)
                got(f"td{h - 1}{p}", src_d)
            if h == 4:
                dst_u, dst_d = tb.at[((z + 5) % 8) // 4, y, c, u], tb.at[((z + 3) % 8) // 4, y, c, d]
            else:
                dst_u, dst_d = ru.at[h - 1, p], rd.at[h - 1, p]
            send(f"tu{h}{p}", src_u, dst_u, up_z)
            send(f"td{h}{p}", src_d, dst_d, dn_z)

    def z_arrived(p):
        got(f"tu4{p}", tb_at(1 - zh, y, c, 64 * p, 32))
        got(f"td4{p}", tb_at(1 - zh, y, c, 64 * p + 32, 32))
        y_send(p + 1)

    line_send(1)
    x_send(0)
    t_hop(1)
    y_send(0)

    def pot_step(k, _):
        row = jnp.broadcast_to(pot_ref[pl.ds(k, 1), :], (128, 128))
        potb[k] = jnp.transpose(row)
        return 0

    lax.fori_loop(0, 16, pot_step, 0)

    def prep_rows(zq, yy):
        hi, lo = halves(jnp.transpose(tb[zq, yy].reshape(256, D)))
        cols = pl.ds(pl.multiple_of((zq * 4 + yy) * 256, 256), 256)
        tth[:, cols] = hi
        ttl[:, cols] = lo

    def split_x(k, _):
        rows = pl.ds(pl.multiple_of(k * 64, 64), 64)
        hi, lo = halves(xg[rows, :])
        xh[rows, :] = hi
        xl[rows, :] = lo
        return 0

    def plan_part(rows_t, pot, put):
        hi, lo = halves(rows_t)
        prod = dot(
            jnp.concatenate([hi, lo, hi], axis=1),
            jnp.concatenate([xh[...], xh[...], xl[...]], axis=0),
        )
        p = jnp.exp(prod[:, :F] * SCALE + jnp.concatenate([pot] * 4, axis=1))
        gd = prod[:, F:]
        put(p, gd)
        acc[0:8, :] += jnp.sum(p.reshape(32, 8, F), axis=0)
        acc[8:16, :] += jnp.sum((p * gd).reshape(32, 8, F), axis=0)

    def plan_block(zq, yy):
        def put(p, gd):
            pm[zq, yy] = p.reshape(2, TB, F)
            gdm[zq, yy] = gd.reshape(2, TB, F)

        pot = potb[pl.ds((zq * 4 + yy) * 2, 2)].reshape(256, 128)
        plan_part(tb[zq, yy].reshape(256, D), pot, put)

    def plan_piece(zq, two_y, p):
        rows = pl.ds(64 * p, 64)

        def put(p_, gd):
            for k, yy in enumerate(two_y):
                part = slice(128 * k, 128 * k + 128)
                pm[zq, yy, :, rows, :] = p_[part].reshape(2, 64, F)
                gdm[zq, yy, :, rows, :] = gd[part].reshape(2, 64, F)

        pot = jnp.concatenate([potb[pl.ds((zq * 4 + yy) * 2, 2), rows, :].reshape(128, 128) for yy in two_y], axis=0)
        tok = jnp.concatenate([tb[zq, yy, :, rows, :].reshape(128, D) for yy in two_y], axis=0)
        plan_part(tok, pot, put)

    def loop(n, step):
        lax.fori_loop(0, n, lambda k, _: (step(k), 0)[1], 0)

    acc[...] = jnp.zeros_like(acc)
    line_step(1)
    x_forward(0)
    t_hop(2)
    y_forward(0)
    line_step(2)
    by_step(1, x_forward)
    t_hop(3)
    y_last(0)
    line_step(3)
    by_step(2, x_forward)
    sib_got(0)
    t_hop(4)
    by_step(3, x_forward)
    loop(4, lambda k: prep_rows(zh, k))
    z_arrived(0)
    z_arrived(1)
    for r in range(4):
        x_last(r)
    for r in (1, 3):
        x_sent(r)
    lax.fori_loop(0, 8, split_x, 0)
    plan_block(zh, 0)
    y_forward(1)
    plan_block(zh, 1)
    y_forward(2)
    loop(2, lambda k: plan_block(zh, k + 2))
    y_last(1)
    sib_got(1, (0, 1))
    plan_piece(1 - zh, (y, ym_), 0)
    y_last(2)
    sib_got(2, (0, 1))
    plan_piece(1 - zh, (y, ym_), 1)
    sib_got(1, (2, 3))
    plan_piece(1 - zh, (yp_, (y + 2) % 4), 0)
    sib_got(2, (2, 3))
    plan_piece(1 - zh, (yp_, (y + 2) % 4), 1)

    mine = st.at[t_me]
    mass_part = jnp.sum(acc[0:8, :], axis=0, keepdims=True)
    dots_part = jnp.sum(acc[8:16, :], axis=0, keepdims=True)
    for k in range(4):
        mine[k : k + 1, :] = mass_part[:, k * 128 : (k + 1) * 128]
        mine[k + 4 : k + 5, :] = dots_part[:, k * 128 : (k + 1) * 128]
    for k in range(1, 16):
        send(f"st{k}", mine, mine, text_peers[k - 1])

    loop(4, lambda k: prep_rows(1 - zh, k))

    def right_x(k, _):
        cols = pl.ds(pl.multiple_of(k * 128, 128), 128)
        hi, lo = halves(jnp.transpose(xg[:, cols]) * SCALE)
        rows = pl.ds(pl.multiple_of(F + k * 128, 128), 128)
        rh[rows, :] = hi
        rl[rows, :] = lo
        return 0

    def right_g(k, _):
        cols = pl.ds(pl.multiple_of(F + k * 128, 128), 128)
        hi, lo = halves(jnp.transpose(xg[:, cols]))
        rows = pl.ds(pl.multiple_of(k * 128, 128), 128)
        rh[rows, :] = hi
        rl[rows, :] = lo
        return 0

    lax.fori_loop(0, 4, right_x, 0)
    lax.fori_loop(0, 4, right_g, 0)

    for k in range(1, 16):
        got(f"st{k}", st.at[(t_me + 16 - k) % 16])
    total = jnp.sum(st[...], axis=0)
    mass = jnp.concatenate([total[k : k + 1, :] for k in range(4)], axis=1)
    inv = 1.0 / mass
    dots = jnp.concatenate([total[k : k + 1, :] for k in range(4, 8)], axis=1) / mass

    def rows_of(q, d):
        zq, yd = zq_of(q), (y + d) % 4
        return zq, yd, pl.ds(pl.multiple_of((zq * 4 + yd) * 256, 256), 256)

    def weigh(q, d):
        zq, yd, rows = rows_of(q, d)
        sh = pm[zq, yd].reshape(256, F) * inv
        w_hi, w_lo = halves(sh * (gdm[zq, yd].reshape(256, F) - dots))
        wh[rows, :] = w_hi
        wl[rows, :] = w_lo
        return sh, w_hi, w_lo

    def text_block(q, d):
        zq, yd, rows = rows_of(q, d)
        if q == 1:
            sh, w_hi, w_lo = weigh(q, d)
        else:
            sh, w_hi, w_lo = pm[zq, yd].reshape(256, F) * inv, wh[rows, :], wl[rows, :]
        sh_hi, sh_lo = halves(sh)
        out = dot(
            jnp.concatenate([sh_hi, w_hi, sh_lo, w_lo, sh_hi, w_hi], axis=1),
            jnp.concatenate([rh[...], rh[...], rl[...]], axis=0),
        )
        cp[zq, yd] = out.reshape(2, TB, D)
        send(f"cs{q}{d}", cp.at[zq, yd, 1 - c], sbuf.at[q, d], sib)

    def chip_sum(q, d):
        got(f"cs{q}{d}", sbuf.at[q, d])
        return cp[zq_of(q), (y + d) % 4, c] + sbuf[q, d]

    def upper(p):
        return pl.ds(64 * p, 32)

    def lower(p):
        return pl.ds(64 * p + 32, 32)

    def far_y():
        ys[0, 2] = chip_sum(0, 2)
        for p in range(2):
            send(f"ra{p}", ys.at[0, 2, upper(p)], ry2.at[p, 0], up_y)
            send(f"rb{p}", ys.at[0, 2, lower(p)], ry2.at[p, 1], dn_y)

    def free_y():
        ys[0, 1] = chip_sum(0, 1)
        ys[0, 3] = chip_sum(0, 3)
        for p in range(2):
            send(f"re{p}", ys.at[0, 1, lower(p)], ry1.at[0, 0, lower(p)], up_y)
            send(f"rf{p}", ys.at[0, 3, upper(p)], ry1.at[0, 1, upper(p)], dn_y)

    def near_y(p):
        got(f"ra{p}", ry2.at[p, 0])
        ys[0, 1, upper(p)] += ry2[p, 0]
        send(f"rc{p}", ys.at[0, 1, upper(p)], ry1.at[0, 0, upper(p)], up_y)
        got(f"rb{p}", ry2.at[p, 1])
        ys[0, 3, lower(p)] += ry2[p, 1]
        send(f"rd{p}", ys.at[0, 3, lower(p)], ry1.at[0, 1, lower(p)], dn_y)

    def own_y(p):
        got(f"re{p}", ry1.at[0, 0, lower(p)])
        got(f"rf{p}", ry1.at[0, 1, upper(p)])
        got(f"rc{p}", ry1.at[0, 0, upper(p)])
        got(f"rd{p}", ry1.at[0, 1, lower(p)])
        rows = pl.ds(64 * p, 64)
        ys[0, 0, rows] += ry1[0, 0, rows] + ry1[0, 1, rows]

    def piece(p):
        return pl.ds(32 * p, 32)

    def straight(name, d, p):
        to, dst = {
            "qf": (dev(zh, (y + 2) % 4, c, zl, x), qfar),
            "qu": (up_y, ry1.at[1, 0]),
            "qd": (dn_y, ry1.at[1, 1]),
        }[name]
        send(f"{name}{p}", ys.at[1, d, piece(p)], dst.at[piece(p)], to)

    def own_z(p):
        rows = piece(p)
        got(f"qf{p}", qfar.at[rows])
        got(f"qu{p}", ry1.at[1, 0, rows])
        got(f"qd{p}", ry1.at[1, 1, rows])
        ys[1, 0, rows] += qfar[rows] + (ry1[1, 0, rows] + ry1[1, 1, rows])
        send(f"w{p}", ys.at[1, 0, rows], zr.at[rows], far_z)

    def speech_rows(m):
        rows = pl.ds(m * 256, 256)
        hi, lo = tth[rows, :], ttl[rows, :]
        out = dot(
            jnp.concatenate([hi, lo, hi], axis=1),
            jnp.concatenate([wh[...], wh[...], wl[...]], axis=0),
        )
        sp[pl.ds(m * 2, 2)] = out.reshape(2, 4, 32, F)

    x2 = (x + 2) % 4
    top, low = pl.ds(0, 16), pl.ds(16, 16)

    def far_x(m):
        two = pl.ds(2 * m, 2)
        send(f"ua{m}", sp.at[two, x2, top], rx2.at[0, two], up_x)
        send(f"ub{m}", sp.at[two, x2, low], rx2.at[1, two], dn_x)
        send(f"ue{m}", sp.at[two, xp_, low], rx1.at[0, two, low], up_x)
        send(f"uf{m}", sp.at[two, xm_, top], rx1.at[1, two, top], dn_x)

    def near_x(m):
        two = pl.ds(2 * m, 2)
        got(f"ua{m}", rx2.at[0, two])
        xs[0, two] = sp[two, xp_, 0:16] + rx2[0, two]
        send(f"uc{m}", xs.at[0, two], rx1.at[0, two, top], up_x)
        got(f"ub{m}", rx2.at[1, two])
        xs[1, two] = sp[two, xm_, 16:32] + rx2[1, two]
        send(f"ud{m}", xs.at[1, two], rx1.at[1, two, low], dn_x)

    def own_x(m):
        two = pl.ds(2 * m, 2)
        got(f"ue{m}", rx1.at[0, two, low])
        got(f"uf{m}", rx1.at[1, two, top])
        got(f"uc{m}", rx1.at[0, two, top])
        got(f"ud{m}", rx1.at[1, two, low])
        xo[two] = sp[two, x] + (rx1[0, two] + rx1[1, two])

    text_block(1, 2)
    text_block(1, 1)
    ys[1, 2] = chip_sum(1, 2)
    straight("qf", 2, 0)
    text_block(1, 3)
    ys[1, 1] = chip_sum(1, 1)
    straight("qu", 1, 0)
    text_block(1, 0)
    ys[1, 3] = chip_sum(1, 3)
    straight("qd", 3, 0)
    for p in range(1, 4):
        straight("qf", 2, p)
        straight("qu", 1, p)
        straight("qd", 3, p)
    loop(4, lambda k: weigh(0, k))
    ys[1, 0] = chip_sum(1, 0)
    speech_rows(0)
    far_x(0)
    text_block(0, 2)
    own_z(0)
    speech_rows(1)
    far_x(1)
    own_z(1)
    text_block(0, 1)
    far_y()
    near_x(0)
    text_block(0, 3)
    own_z(2)
    near_x(1)
    text_block(0, 0)
    free_y()
    own_z(3)
    own_x(0)
    near_y(0)
    near_y(1)
    own_x(1)
    for r in (1, 2, 3):
        zt = (zl + r) % 4
        send(f"v{r}", xo.at[zt], rz.at[r - 1], dev(zh, y, c, zt, x))
    ys[0, 0] = chip_sum(0, 0)
    own_y(0)
    own_y(1)
    for p in range(4):
        got(f"w{p}", zr.at[piece(p)])
    tg_ref[...] = ys[0, 0] + zr[...]
    for r in (1, 2, 3):
        got(f"v{r}", rz.at[r - 1])
    sg_ref[...] = (xo[zl] + (rz[0] + (rz[1] + rz[2]))) * SCALE
    for j in (1, 2, 3):
        for fits, one in (line_up(j), line_down(j)):

            @pl.when(fits)
            def _(one=one):
                one.wait_send()

    for one in pending:
        one.wait_send()


def finish(sg_ref, tg_ref, sg_out, tg_out):
    sg_out[...] = sg_ref[...]
    tg_out[...] = tg_ref[...]


def solution(mesh):
    def v(shape, kind=F32):
        return pltpu.VMEM(shape, kind)

    scratch = [
        v((D, 2 * F)), v((2, 4, 2, TB, D)), v((D, 2 * F), BF), v((D, 2 * F), BF),
        v((D, T), BF), v((D, T), BF), v((2 * F, D), BF), v((2 * F, D), BF),
        v((16, TB, 128)), v((2, 4, 2, TB, F)), v((2, 4, 2, TB, F)), v((T, F), BF), v((T, F), BF), v((16, F)), v((16, 8, 128)),
        v((2, 4, 2, TB, D)), v((2, 4, TB, D)), v((2, 4, TB, D)), v((2, 2, 32, D)), v((2, 2, TB, D)), v((TB, D)),
        v((TB, D)), v((3, 2, 32, D)), v((3, 2, 32, D)),
        v((4, 4, 32, F)), v((2, 4, 16, F)), v((4, 32, F)), v((2, 4, 16, F)), v((2, 4, 32, F)), v((3, 32, F)),
        pltpu.SemaphoreType.DMA((len(NAMES),)),
        pltpu.SemaphoreType.DMA((len(NAMES),)),
        pltpu.SemaphoreType.DMA((3,)),
    ]
    anywhere = pl.BlockSpec(memory_space=pl.ANY)
    vmem = pl.BlockSpec(memory_space=pltpu.VMEM)
    call = pl.pallas_call(
        kernel,
        out_shape=(jax.ShapeDtypeStruct((32, F), F32), jax.ShapeDtypeStruct((TB, D), F32)),
        in_specs=[anywhere, anywhere, anywhere, vmem],
        out_specs=(vmem, vmem),
        scratch_shapes=scratch,
        compiler_params=pltpu.CompilerParams(
            collective_id=0, has_side_effects=True, vmem_limit_bytes=62 * 1024 * 1024
        ),
    )

    last = pl.pallas_call(
        finish,
        out_shape=(jax.ShapeDtypeStruct((32, F), F32), jax.ShapeDtypeStruct((TB, D), F32)),
        in_specs=[vmem, vmem],
        out_specs=(vmem, vmem),
    )

    def shards(speech_feat, text_feat, text_pot, map_grad):
        sg, tg = last(*call(speech_feat.T, map_grad.T, text_feat, text_pot.reshape(16, 128)))
        return sg.T, tg

    return jax.shard_map(
        shards,
        mesh=mesh,
        in_specs=(P("speech", "text"), P(("text", "speech"), None), P("text"), P("speech", "text")),
        out_specs=(P("speech", "text"), P(("text", "speech"), None)),
        check_vma=False,
    )
```

```python
import math

import jax
import jax.numpy as jnp
from jax import lax
from jax.experimental import pallas as pl
from jax.experimental.pallas import tpu as pltpu
from jax.sharding import PartitionSpec as P

D = 512
F = 512
T = 2048
TB = 128
SCALE = 1.0 / math.sqrt(D)
BF = jnp.bfloat16
F32 = jnp.float32
MESH = pl.DeviceIdType.MESH

GROUPS = (
    ["xf", "st", "v", "w", "sb0"]
    + [f"x{r}" for r in range(4)]
    + [f"z{k}{j}" for k in "ud" for j in (1, 2, 3)]
    + [f"t{h}{p}" for h in (1, 2, 3, 4) for p in range(4)]
    + [f"{k}{g}" for g in range(5) for k in ("y", "yf", "sbn", "sbf") if g or k[0] == "y"]
    + [f"{k}{p}" for p in range(4) for k in ("cs", "ct")]
    + [f"{k}{p}" for p in range(2) for k in ("ra", "rb", "ua", "ub")]
    + [f"q{n}" for n in range(5)]
)
KINDS = ["x", "t", "y", "yy", "st", "c", "r", "q", "u", "v"] + [f"z{k}{j}" for k in "ud" for j in (1, 2, 3)]
GROUP = {name: k for k, name in enumerate(GROUPS)}
KIND = {name: k for k, name in enumerate(KINDS)}
PARTS = ((0, 16), (16, 16), (32, 32), (64, 32), (96, 32))


def halves(v):
    hi = v.astype(BF)
    return hi, (v - hi.astype(F32)).astype(BF)


def dot(a, b):
    return lax.dot_general(a, b, (((1,), (0,)), ((), ())), preferred_element_type=F32)


def kernel(
    x_ref, g_ref, t_ref, pot_ref, sg_ref, tg_ref,
    xg, tb, xh, xl, tth, ttl, rh, rl, potb, pm, gdm, wh, wl, acc, st,
    cp, sbuf, ys, ry2, ry1, qfar, zr, ru, rd,
    sp, xs, xo, rx2, rx1, rz,
    ssem, rsem, lsem,
):
    s_me = lax.axis_index("speech")
    t_me = lax.axis_index("text")
    zh, y, c = s_me // 8, (s_me // 2) % 4, s_me % 2
    zl, x = t_me // 4, t_me % 4
    z = zh * 4 + zl

    def dev(zh_, y_, c_, zl_, x_):
        return {"speech": (zh_ * 4 + y_) * 2 + c_, "text": zl_ * 4 + x_}

    def at_z(zz):
        return dev(zz // 4, y, c, zz % 4, x)

    yp_, ym_ = (y + 1) % 4, (y + 3) % 4
    xp_, xm_ = (x + 1) % 4, (x + 3) % 4
    sib = dev(zh, y, 1 - c, zl, x)
    up_y, dn_y = dev(zh, yp_, c, zl, x), dev(zh, ym_, c, zl, x)
    up_x, dn_x = dev(zh, y, c, zl, xp_), dev(zh, y, c, zl, xm_)
    far_z = at_z((z + 4) % 8)
    up_z, dn_z = at_z((z + 1) % 8), at_z((z + 7) % 8)

    sent = dict.fromkeys(KINDS, 0)

    def copy(kind, group, src, dst, to):
        return pltpu.make_async_remote_copy(
            src_ref=src,
            dst_ref=dst,
            send_sem=ssem.at[KIND[kind]],
            recv_sem=rsem.at[GROUP[group]],
            device_id=to,
            device_id_type=MESH,
        )

    def send(kind, group, src, dst, to, track=True):
        copy(kind, group, src, dst, to).start()
        if track:
            sent[kind] += math.prod(src.shape) * 4

    def bulk(size):
        return st.at[pl.ds(0, 15)] if size == 61440 else xg.at[pl.ds(0, size // 4096), :]

    def got(group, ref):
        copy("x", group, ref, ref, sib).wait_recv()

    def got_kb(group, kb):
        got(group, bulk(kb * 1024))

    def xg_at(zl_, x_, lo=0, n=32):
        return xg.at[pl.ds(pl.multiple_of((zl_ * 4 + x_) * 32 + lo, 16), n), :]

    def tb_at(zh_, y_, c_, lo=0, n=TB):
        return tb.at[zh_, y_, c_, pl.ds(lo, n), :]

    own_rows = pl.ds(pl.multiple_of(t_me * 32, 32), 32)
    local = [
        pltpu.make_async_copy(x_ref, xg.at[own_rows, pl.ds(0, F)], lsem.at[0]),
        pltpu.make_async_copy(g_ref, xg.at[own_rows, pl.ds(F, F)], lsem.at[1]),
        pltpu.make_async_copy(t_ref, tb_at(zh, y, c), lsem.at[2]),
    ]
    for one in local:
        one.start()
    barrier = pltpu.get_barrier_semaphore()
    text_peers = [{"speech": s_me, "text": (t_me + k) % 16} for k in range(1, 16)]
    for to in (sib, up_y, dn_y, up_x, dn_x, up_z, dn_z):
        pl.semaphore_signal(barrier, inc=1, device_id=to, device_id_type=MESH)
    for one in local:
        one.wait()
    pl.semaphore_wait(barrier, 7)

    def line_up(j):
        block = xg_at(zl + 1 - j, x)
        return (zl <= 2) & (zl >= j - 1), copy(f"zu{j}", f"zu{j}", block, block, dev(zh, y, c, zl + 1, x))

    def line_down(j):
        block = xg_at(zl + j - 1, x)
        return (zl >= 1) & (zl <= 4 - j), copy(f"zd{j}", f"zd{j}", block, block, dev(zh, y, c, zl - 1, x))

    def line_send(j):
        for fits, one in (line_up(j), line_down(j)):

            @pl.when(fits)
            def _(one=one):
                one.start()

    def line_got(j):
        @pl.when(zl >= j)
        def _():
            got(f"zu{j}", xg_at(zl - j, x))

        @pl.when(zl <= 3 - j)
        def _():
            got(f"zd{j}", xg_at(zl + j, x))

    def line_step(j):
        line_got(j)
        if j < 3:
            line_send(j + 1)
        by_step(j, x_send)

    def by_step(j, do):
        if j == 2:
            do(2)
            return
        for r, here in ((1, zl >= 1), (3, zl <= 2)) if j == 1 else ((3, zl == 3), (1, zl == 0)):

            @pl.when(here)
            def _(r=r):
                do(r, False)

    def x_send(r, track=True):
        zs = (zl + 4 - r) % 4
        send("x", f"x{r}", xg_at(zs, x), xg_at(zs, x), up_x, track)
        send("x", f"x{r}", xg_at(zs, x), xg_at(zs, x), dn_x, track)

    def x_forward(r, track=True):
        zs = (zl + 4 - r) % 4
        got_kb(f"x{r}", 256)
        send("x", "xf", xg_at(zs, xm_, 0, 16), xg_at(zs, xm_, 0, 16), up_x, track)
        send("x", "xf", xg_at(zs, xp_, 16, 16), xg_at(zs, xp_, 16, 16), dn_x, track)

    def zq_of(q):
        return zh if q == 0 else 1 - zh

    def parcel(g):
        return (zh, 0, TB) if g == 0 else (1 - zh, (g - 1) * 32, 32)

    def yk(g):
        return "yy" if g else "y"

    def sb(g, k):
        return "sb0" if g == 0 else f"sbf{g}" if k > 1 else f"sbn{g}"

    def y_send(g):
        zq, lo, n = parcel(g)
        send(yk(g), f"y{g}", tb_at(zq, y, c, lo, n), tb_at(zq, y, c, lo, n), up_y)
        send(yk(g), f"y{g}", tb_at(zq, y, c, lo, n), tb_at(zq, y, c, lo, n), dn_y)
        send(yk(g), sb(g, 0), tb_at(zq, y, c, lo, n), tb_at(zq, y, c, lo, n), sib)

    def y_forward(g):
        zq, lo, n = parcel(g)
        h = n // 2
        got_kb(f"y{g}", 4 * n)
        send(yk(g), f"yf{g}", tb_at(zq, ym_, c, lo, h), tb_at(zq, ym_, c, lo, h), up_y)
        send(yk(g), f"yf{g}", tb_at(zq, yp_, c, lo + h, h), tb_at(zq, yp_, c, lo + h, h), dn_y)
        send(yk(g), sb(g, 1), tb_at(zq, ym_, c, lo, n), tb_at(zq, ym_, c, lo, n), sib)
        send(yk(g), sb(g, 2), tb_at(zq, yp_, c, lo, n), tb_at(zq, yp_, c, lo, n), sib)

    def y_last(g):
        zq, lo, n = parcel(g)
        h, y2 = n // 2, (y + 2) % 4
        got(f"yf{g}", tb_at(zq, y2, c, lo, n))
        send(yk(g), sb(g, 3), tb_at(zq, y2, c, lo, n), tb_at(zq, y2, c, lo, n), sib)

    def sib_got(g, far=False):
        if g == 0:
            got_kb("sb0", 1024)
        else:
            got_kb(sb(g, 2 if far else 0), 128)

    def t_hop(h):
        for p in range(4):
            u, d = pl.ds(32 * p, 16), pl.ds(32 * p + 16, 16)
            if h == 1:
                src_u, src_d = tb.at[zh, y, c, u], tb.at[zh, y, c, d]
            else:
                src_u, src_d = ru.at[h - 2, p], rd.at[h - 2, p]
                got_kb(f"t{h - 1}{p}", 64)
            if h == 4:
                dst_u, dst_d = tb.at[((z + 5) % 8) // 4, y, c, u], tb.at[((z + 3) % 8) // 4, y, c, d]
            else:
                dst_u, dst_d = ru.at[h - 1, p], rd.at[h - 1, p]
            send("t", f"t{h}{p}", src_u, dst_u, up_z)
            send("t", f"t{h}{p}", src_d, dst_d, dn_z)

    def z_arrived(p):
        got(f"t4{p}", tb_at(1 - zh, y, c, 32 * p, 32))
        y_send(p + 1)

    line_send(1)
    x_send(0)
    t_hop(1)
    y_send(0)

    def pot_step(k, _):
        row = jnp.broadcast_to(pot_ref[pl.ds(k, 1), :], (128, 128))
        potb[k] = jnp.transpose(row)
        return 0

    lax.fori_loop(0, 16, pot_step, 0)

    def prep_rows(zq, yy):
        hi, lo = halves(jnp.transpose(tb[zq, yy].reshape(256, D)))
        cols = pl.ds(pl.multiple_of((zq * 4 + yy) * 256, 256), 256)
        tth[:, cols] = hi
        ttl[:, cols] = lo

    def split_x(k, _):
        rows = pl.ds(pl.multiple_of(k * 64, 64), 64)
        hi, lo = halves(xg[rows, :])
        xh[rows, :] = hi
        xl[rows, :] = lo
        return 0

    def plan_part(rows_t, pot, put):
        hi, lo = halves(rows_t)
        prod = dot(
            jnp.concatenate([hi, lo, hi], axis=1),
            jnp.concatenate([xh[...], xh[...], xl[...]], axis=0),
        )
        p = jnp.exp(prod[:, :F] * SCALE + jnp.concatenate([pot] * 4, axis=1))
        gd = prod[:, F:]
        put(p, gd)
        acc[0:8, :] += jnp.sum(p.reshape(32, 8, F), axis=0)
        acc[8:16, :] += jnp.sum((p * gd).reshape(32, 8, F), axis=0)

    def plan_block(zq, yy):
        def put(p, gd):
            pm[zq, yy] = p.reshape(2, TB, F)
            gdm[zq, yy] = gd.reshape(2, TB, F)

        pot = potb[pl.ds((zq * 4 + yy) * 2, 2)].reshape(256, 128)
        plan_part(tb[zq, yy].reshape(256, D), pot, put)

    def plan_piece(zq, two_y, p):
        rows = pl.ds(64 * p, 64)

        def put(p_, gd):
            for k, yy in enumerate(two_y):
                part = slice(128 * k, 128 * k + 128)
                pm[zq, yy, :, rows, :] = p_[part].reshape(2, 64, F)
                gdm[zq, yy, :, rows, :] = gd[part].reshape(2, 64, F)

        pot = jnp.concatenate([potb[pl.ds((zq * 4 + yy) * 2, 2), rows, :].reshape(128, 128) for yy in two_y], axis=0)
        tok = jnp.concatenate([tb[zq, yy, :, rows, :].reshape(128, D) for yy in two_y], axis=0)
        plan_part(tok, pot, put)

    def loop(n, step):
        lax.fori_loop(0, n, lambda k, _: (step(k), 0)[1], 0)

    acc[...] = jnp.zeros_like(acc)
    line_step(1)
    x_forward(0)
    t_hop(2)
    y_forward(0)
    line_step(2)
    by_step(1, x_forward)
    t_hop(3)
    y_last(0)
    line_step(3)
    by_step(2, x_forward)
    sib_got(0)
    t_hop(4)
    by_step(3, x_forward)
    loop(4, lambda k: prep_rows(zh, k))
    z_arrived(0)
    z_arrived(1)
    z_arrived(2)
    z_arrived(3)
    got_kb("xf", 512)
    lax.fori_loop(0, 8, split_x, 0)
    plan_block(zh, 0)
    y_forward(1)
    plan_block(zh, 1)
    y_forward(2)
    plan_block(zh, 2)
    y_forward(3)
    plan_block(zh, 3)
    y_forward(4)
    sib_got(1)
    sib_got(2)
    plan_piece(1 - zh, (y, ym_), 0)
    y_last(1)
    y_last(2)
    sib_got(3)
    sib_got(4)
    plan_piece(1 - zh, (y, ym_), 1)
    y_last(3)
    y_last(4)
    sib_got(1, True)
    sib_got(2, True)
    plan_piece(1 - zh, (yp_, (y + 2) % 4), 0)
    sib_got(3, True)
    sib_got(4, True)
    plan_piece(1 - zh, (yp_, (y + 2) % 4), 1)

    mine = st.at[t_me]
    mass_part = jnp.sum(acc[0:8, :], axis=0, keepdims=True)
    dots_part = jnp.sum(acc[8:16, :], axis=0, keepdims=True)
    for k in range(4):
        mine[k : k + 1, :] = mass_part[:, k * 128 : (k + 1) * 128]
        mine[k + 4 : k + 5, :] = dots_part[:, k * 128 : (k + 1) * 128]
    for k in range(1, 16):
        send("st", "st", mine, mine, text_peers[k - 1])

    loop(4, lambda k: prep_rows(1 - zh, k))

    def right_x(k, _):
        cols = pl.ds(pl.multiple_of(k * 128, 128), 128)
        hi, lo = halves(jnp.transpose(xg[:, cols]) * SCALE)
        rows = pl.ds(pl.multiple_of(F + k * 128, 128), 128)
        rh[rows, :] = hi
        rl[rows, :] = lo
        return 0

    def right_g(k, _):
        cols = pl.ds(pl.multiple_of(F + k * 128, 128), 128)
        hi, lo = halves(jnp.transpose(xg[:, cols]))
        rows = pl.ds(pl.multiple_of(k * 128, 128), 128)
        rh[rows, :] = hi
        rl[rows, :] = lo
        return 0

    lax.fori_loop(0, 4, right_x, 0)
    lax.fori_loop(0, 4, right_g, 0)

    got_kb("st", 60)
    total = jnp.sum(st[...], axis=0)
    mass = jnp.concatenate([total[k : k + 1, :] for k in range(4)], axis=1)
    inv = 1.0 / mass
    dots = jnp.concatenate([total[k : k + 1, :] for k in range(4, 8)], axis=1) / mass

    def weights(p, gd):
        sh = p * inv
        return halves(sh), halves(sh * (gd - dots))

    def right_product(sh, w):
        return dot(
            jnp.concatenate([sh[0], w[0], sh[1], w[1], sh[0], w[0]], axis=1),
            jnp.concatenate([rh[...], rh[...], rl[...]], axis=0),
        )

    def weigh(yy):
        _, w = weights(pm[zh, yy].reshape(256, F), gdm[zh, yy].reshape(256, F))
        wh[zh, yy] = w[0].reshape(2, TB, F)
        wl[zh, yy] = w[1].reshape(2, TB, F)

    def text_block(d):
        yd = (y + d) % 4
        sh = halves(pm[zh, yd].reshape(256, F) * inv)
        out = right_product(sh, (wh[zh, yd].reshape(256, F), wl[zh, yd].reshape(256, F)))
        cp[zh, yd] = out.reshape(2, TB, D)
        send("c", f"cs{d}", cp.at[zh, yd, 1 - c], sbuf.at[0, d], sib)

    def chip_sum(d):
        got(f"cs{d}", sbuf.at[0, d])
        return cp[zh, (y + d) % 4, c] + sbuf[0, d]

    def piece(p):
        return pl.ds(32 * p, 32)

    def text_piece(p):
        zq, rows = 1 - zh, piece(p)
        sh, w = weights(pm[zq, :, :, rows, :].reshape(256, F), gdm[zq, :, :, rows, :].reshape(256, F))
        wh[zq, :, :, rows, :] = w[0].reshape(4, 2, 32, F)
        wl[zq, :, :, rows, :] = w[1].reshape(4, 2, 32, F)
        cp[zq, :, :, rows, :] = right_product(sh, w).reshape(4, 2, 32, D)
        send("c", f"ct{p}", cp.at[zq, :, 1 - c, rows], sbuf.at[1, :, rows], sib)

    def straight(p):
        rows = piece(p)
        got(f"ct{p}", sbuf.at[1, :, rows])
        ys[1, :, rows] = cp[1 - zh, :, c, rows] + sbuf[1, :, rows]
        y2 = (y + 2) % 4
        for n in (0, 1) if p == 0 else (p + 1,):
            rows = pl.ds(*PARTS[n])
            send("q", f"q{n}", ys.at[1, y2, rows], qfar.at[rows], dev(zh, y2, c, zl, x))
            send("q", f"q{n}", ys.at[1, yp_, rows], ry1.at[1, 0, rows], up_y)
            send("q", f"q{n}", ys.at[1, ym_, rows], ry1.at[1, 1, rows], dn_y)

    def own_z(n):
        rows = pl.ds(*PARTS[n])
        got_kb(f"q{n}", 6 * PARTS[n][1])
        ys[1, y, rows] += qfar[rows] + (ry1[1, 0, rows] + ry1[1, 1, rows])
        send("q", "w", ys.at[1, y, rows], zr.at[rows], far_z)

    def upper(p):
        return pl.ds(64 * p, 32)

    def lower(p):
        return pl.ds(64 * p + 32, 32)

    def far_y():
        ys[0, 2] = chip_sum(2)
        for p in range(2):
            send("r", f"ra{p}", ys.at[0, 2, upper(p)], ry2.at[p, 0], up_y)
            send("r", f"ra{p}", ys.at[0, 2, lower(p)], ry2.at[p, 1], dn_y)

    def free_y():
        ys[0, 1] = chip_sum(1)
        ys[0, 3] = chip_sum(3)
        for p in range(2):
            send("r", f"rb{p}", ys.at[0, 1, lower(p)], ry1.at[0, 0, lower(p)], up_y)
            send("r", f"rb{p}", ys.at[0, 3, upper(p)], ry1.at[0, 1, upper(p)], dn_y)

    def near_y(p):
        got_kb(f"ra{p}", 128)
        ys[0, 1, upper(p)] += ry2[p, 0]
        send("r", f"rb{p}", ys.at[0, 1, upper(p)], ry1.at[0, 0, upper(p)], up_y)
        ys[0, 3, lower(p)] += ry2[p, 1]
        send("r", f"rb{p}", ys.at[0, 3, lower(p)], ry1.at[0, 1, lower(p)], dn_y)

    def own_y(p):
        got_kb(f"rb{p}", 256)
        rows = pl.ds(64 * p, 64)
        ys[0, 0, rows] += ry1[0, 0, rows] + ry1[0, 1, rows]

    def speech_rows(m):
        rows = pl.ds(m * 256, 256)
        hi, lo = tth[rows, :], ttl[rows, :]
        out = dot(
            jnp.concatenate([hi, lo, hi], axis=1),
            jnp.concatenate([wh[...].reshape(T, F), wh[...].reshape(T, F), wl[...].reshape(T, F)], axis=0),
        )
        sp[pl.ds(m * 2, 2)] = out.reshape(2, 4, 32, F)

    x2 = (x + 2) % 4
    top, low = pl.ds(0, 16), pl.ds(16, 16)

    def far_x(m):
        two = pl.ds(2 * m, 2)
        send("u", f"ua{m}", sp.at[two, x2, top], rx2.at[0, two], up_x)
        send("u", f"ua{m}", sp.at[two, x2, low], rx2.at[1, two], dn_x)
        send("u", f"ub{m}", sp.at[two, xp_, low], rx1.at[0, two, low], up_x)
        send("u", f"ub{m}", sp.at[two, xm_, top], rx1.at[1, two, top], dn_x)

    def near_x(m):
        two = pl.ds(2 * m, 2)
        got_kb(f"ua{m}", 128)
        xs[0, two] = sp[two, xp_, 0:16] + rx2[0, two]
        send("u", f"ub{m}", xs.at[0, two], rx1.at[0, two, top], up_x)
        xs[1, two] = sp[two, xm_, 16:32] + rx2[1, two]
        send("u", f"ub{m}", xs.at[1, two], rx1.at[1, two, low], dn_x)

    def own_x(m):
        two = pl.ds(2 * m, 2)
        got_kb(f"ub{m}", 256)
        xo[two] = sp[two, x] + (rx1[0, two] + rx1[1, two])

    text_piece(0)
    text_piece(1)
    straight(0)
    text_piece(2)
    straight(1)
    text_piece(3)
    straight(2)
    loop(4, weigh)
    straight(3)
    own_z(0)
    speech_rows(0)
    far_x(0)
    own_z(1)
    speech_rows(1)
    far_x(1)
    text_block(2)
    own_z(2)
    text_block(1)
    far_y()
    near_x(0)
    text_block(3)
    own_z(3)
    near_x(1)
    text_block(0)
    free_y()
    own_z(4)
    own_x(0)
    own_x(1)
    for r in (1, 2, 3):
        zt = (zl + r) % 4
        send("v", "v", xo.at[zt], rz.at[r - 1], dev(zh, y, c, zt, x))
    ys[0, 0] = chip_sum(0)
    near_y(0)
    near_y(1)
    own_y(0)
    own_y(1)
    got("w", zr)
    tg_ref[...] = ys[0, 0] + zr[...]
    got("v", rz)
    sg_ref[...] = (xo[zl] + (rz[0] + (rz[1] + rz[2]))) * SCALE
    for j in (1, 2, 3):
        for fits, one in (line_up(j), line_down(j)):

            @pl.when(fits)
            def _(one=one):
                one.wait_send()

    for r in (1, 3):
        sent["x"] += 2 * 32 * 4096 + 2 * 16 * 4096
    for kind, size in sent.items():
        if size:
            copy(kind, "x0", bulk(size), bulk(size), sib).wait_send()


def finish(sg_ref, tg_ref, sg_out, tg_out):
    sg_out[...] = sg_ref[...]
    tg_out[...] = tg_ref[...]


def solution(mesh):
    def v(shape, kind=F32):
        return pltpu.VMEM(shape, kind)

    scratch = [
        v((D, 2 * F)), v((2, 4, 2, TB, D)), v((D, 2 * F), BF), v((D, 2 * F), BF),
        v((D, T), BF), v((D, T), BF), v((2 * F, D), BF), v((2 * F, D), BF),
        v((16, TB, 128)), v((2, 4, 2, TB, F)), v((2, 4, 2, TB, F)), v((2, 4, 2, TB, F), BF), v((2, 4, 2, TB, F), BF), v((16, F)), v((16, 8, 128)),
        v((2, 4, 2, TB, D)), v((2, 4, TB, D)), v((2, 4, TB, D)), v((2, 2, 32, D)), v((2, 2, TB, D)), v((TB, D)),
        v((TB, D)), v((3, 4, 16, D)), v((3, 4, 16, D)),
        v((4, 4, 32, F)), v((2, 4, 16, F)), v((4, 32, F)), v((2, 4, 16, F)), v((2, 4, 32, F)), v((3, 32, F)),
        pltpu.SemaphoreType.DMA((len(KINDS),)),
        pltpu.SemaphoreType.DMA((len(GROUPS),)),
        pltpu.SemaphoreType.DMA((3,)),
    ]
    anywhere = pl.BlockSpec(memory_space=pl.ANY)
    vmem = pl.BlockSpec(memory_space=pltpu.VMEM)
    call = pl.pallas_call(
        kernel,
        out_shape=(jax.ShapeDtypeStruct((32, F), F32), jax.ShapeDtypeStruct((TB, D), F32)),
        in_specs=[anywhere, anywhere, anywhere, vmem],
        out_specs=(vmem, vmem),
        scratch_shapes=scratch,
        compiler_params=pltpu.CompilerParams(
            collective_id=0, has_side_effects=True, vmem_limit_bytes=62 * 1024 * 1024
        ),
    )

    last = pl.pallas_call(
        finish,
        out_shape=(jax.ShapeDtypeStruct((32, F), F32), jax.ShapeDtypeStruct((TB, D), F32)),
        in_specs=[vmem, vmem],
        out_specs=(vmem, vmem),
    )

    def shards(speech_feat, text_feat, text_pot, map_grad):
        sg, tg = last(*call(speech_feat.T, map_grad.T, text_feat, text_pot.reshape(16, 128)))
        return sg.T, tg

    return jax.shard_map(
        shards,
        mesh=mesh,
        in_specs=(P("speech", "text"), P(("text", "speech"), None), P("text"), P("speech", "text")),
        out_specs=(P("speech", "text"), P(("text", "speech"), None)),
        check_vma=False,
    )
```

```python
import math

import jax
import jax.numpy as jnp
from jax import lax
from jax.experimental import pallas as pl
from jax.experimental.pallas import tpu as pltpu
from jax.sharding import PartitionSpec as P

D = 512
F = 512
T = 2048
TB = 128
SCALE = 1.0 / math.sqrt(D)
BF = jnp.bfloat16
F32 = jnp.float32
MESH = pl.DeviceIdType.MESH

GROUPS = (
    ["xf", "st", "v", "w", "sb0"]
    + [f"x{r}" for r in range(4)]
    + [f"z{k}{j}" for k in "ud" for j in (1, 2, 3)]
    + [f"t{h}{p}" for h in (1, 2, 3, 4) for p in range(4)]
    + [f"{k}{g}" for g in range(5) for k in ("y", "yf", "sbn", "sbf") if g or k[0] == "y"]
    + [f"{k}{p}" for p in range(4) for k in ("cs", "ct")]
    + [f"{k}{p}" for p in range(2) for k in ("ra", "rb", "ua", "ub")]
    + [f"q{n}" for n in range(5)]
)
KINDS = ["x", "t", "y", "yy", "st", "c", "r", "q", "u", "v"] + [f"z{k}{j}" for k in "ud" for j in (1, 2, 3)]
GROUP = {name: k for k, name in enumerate(GROUPS)}
KIND = {name: k for k, name in enumerate(KINDS)}
PARTS = ((0, 16), (16, 16), (32, 32), (64, 32), (96, 32))


def halves(v):
    hi = v.astype(BF)
    return hi, (v - hi.astype(F32)).astype(BF)


def dot(a, b):
    return lax.dot_general(a, b, (((1,), (0,)), ((), ())), preferred_element_type=F32)


def kernel(
    x_ref, g_ref, t_ref, pot_ref, sg_ref, tg_ref,
    xg, tb, xh, xl, tth, ttl, rh, rl, potb, pm, gdm, wh, wl, acc, st,
    cp, sbuf, ys, ry2, ry1, qfar, zr, ru, rd,
    sp, xs, xo, rx2, rx1, rz,
    ssem, rsem, lsem,
):
    s_me = lax.axis_index("speech")
    t_me = lax.axis_index("text")
    zh, y, c = s_me // 8, (s_me // 2) % 4, s_me % 2
    zl, x = t_me // 4, t_me % 4
    z = zh * 4 + zl

    def dev(zh_, y_, c_, zl_, x_):
        return {"speech": (zh_ * 4 + y_) * 2 + c_, "text": zl_ * 4 + x_}

    def at_z(zz):
        return dev(zz // 4, y, c, zz % 4, x)

    yp_, ym_ = (y + 1) % 4, (y + 3) % 4
    xp_, xm_ = (x + 1) % 4, (x + 3) % 4
    sib = dev(zh, y, 1 - c, zl, x)
    up_y, dn_y = dev(zh, yp_, c, zl, x), dev(zh, ym_, c, zl, x)
    up_x, dn_x = dev(zh, y, c, zl, xp_), dev(zh, y, c, zl, xm_)
    far_z = at_z((z + 4) % 8)
    up_z, dn_z = at_z((z + 1) % 8), at_z((z + 7) % 8)

    sent = dict.fromkeys(KINDS, 0)

    def copy(kind, group, src, dst, to):
        return pltpu.make_async_remote_copy(
            src_ref=src,
            dst_ref=dst,
            send_sem=ssem.at[KIND[kind]],
            recv_sem=rsem.at[GROUP[group]],
            device_id=to,
            device_id_type=MESH,
        )

    def send(kind, group, src, dst, to, track=True):
        copy(kind, group, src, dst, to).start()
        if track:
            sent[kind] += math.prod(src.shape) * 4

    def bulk(size):
        return st.at[pl.ds(0, 15)] if size == 61440 else xg.at[pl.ds(0, size // 4096), :]

    def got(group, ref):
        copy("x", group, ref, ref, sib).wait_recv()

    def got_kb(group, kb):
        got(group, bulk(kb * 1024))

    def xg_at(zl_, x_, lo=0, n=32):
        return xg.at[pl.ds(pl.multiple_of((zl_ * 4 + x_) * 32 + lo, 16), n), :]

    def tb_at(zh_, y_, c_, lo=0, n=TB):
        return tb.at[zh_, y_, c_, pl.ds(lo, n), :]

    own_rows = pl.ds(pl.multiple_of(t_me * 32, 32), 32)
    local = [
        pltpu.make_async_copy(x_ref, xg.at[own_rows, pl.ds(0, F)], lsem.at[0]),
        pltpu.make_async_copy(g_ref, xg.at[own_rows, pl.ds(F, F)], lsem.at[1]),
        pltpu.make_async_copy(t_ref, tb_at(zh, y, c), lsem.at[2]),
    ]
    for one in local:
        one.start()
    barrier = pltpu.get_barrier_semaphore()
    text_peers = [{"speech": s_me, "text": (t_me + k) % 16} for k in range(1, 16)]
    for to in (sib, up_y, dn_y, up_x, dn_x, up_z, dn_z):
        pl.semaphore_signal(barrier, inc=1, device_id=to, device_id_type=MESH)
    for one in local:
        one.wait()
    pl.semaphore_wait(barrier, 7)

    def line_up(j):
        block = xg_at(zl + 1 - j, x)
        return (zl <= 2) & (zl >= j - 1), copy(f"zu{j}", f"zu{j}", block, block, dev(zh, y, c, zl + 1, x))

    def line_down(j):
        block = xg_at(zl + j - 1, x)
        return (zl >= 1) & (zl <= 4 - j), copy(f"zd{j}", f"zd{j}", block, block, dev(zh, y, c, zl - 1, x))

    def line_send(j):
        for fits, one in (line_up(j), line_down(j)):

            @pl.when(fits)
            def _(one=one):
                one.start()

    def line_got(j):
        @pl.when(zl >= j)
        def _():
            got(f"zu{j}", xg_at(zl - j, x))

        @pl.when(zl <= 3 - j)
        def _():
            got(f"zd{j}", xg_at(zl + j, x))

    def line_step(j):
        line_got(j)
        if j < 3:
            line_send(j + 1)
        by_step(j, x_send)

    def by_step(j, do):
        if j == 2:
            do(2)
            return
        for r, here in ((1, zl >= 1), (3, zl <= 2)) if j == 1 else ((3, zl == 3), (1, zl == 0)):

            @pl.when(here)
            def _(r=r):
                do(r, False)

    def x_send(r, track=True):
        zs = (zl + 4 - r) % 4
        send("x", f"x{r}", xg_at(zs, x), xg_at(zs, x), up_x, track)
        send("x", f"x{r}", xg_at(zs, x), xg_at(zs, x), dn_x, track)

    def x_forward(r, track=True):
        zs = (zl + 4 - r) % 4
        got_kb(f"x{r}", 256)
        send("x", "xf", xg_at(zs, xm_, 0, 16), xg_at(zs, xm_, 0, 16), up_x, track)
        send("x", "xf", xg_at(zs, xp_, 16, 16), xg_at(zs, xp_, 16, 16), dn_x, track)

    def zq_of(q):
        return zh if q == 0 else 1 - zh

    def parcel(g):
        return (zh, 0, TB) if g == 0 else (1 - zh, (g - 1) * 32, 32)

    def yk(g):
        return "yy" if g else "y"

    def sb(g, k):
        return "sb0" if g == 0 else f"sbf{g}" if k > 1 else f"sbn{g}"

    def y_send(g):
        zq, lo, n = parcel(g)
        send(yk(g), f"y{g}", tb_at(zq, y, c, lo, n), tb_at(zq, y, c, lo, n), up_y)
        send(yk(g), f"y{g}", tb_at(zq, y, c, lo, n), tb_at(zq, y, c, lo, n), dn_y)
        send(yk(g), sb(g, 0), tb_at(zq, y, c, lo, n), tb_at(zq, y, c, lo, n), sib)

    def y_forward(g):
        zq, lo, n = parcel(g)
        h = n // 2
        got_kb(f"y{g}", 4 * n)
        send(yk(g), f"yf{g}", tb_at(zq, ym_, c, lo, h), tb_at(zq, ym_, c, lo, h), up_y)
        send(yk(g), f"yf{g}", tb_at(zq, yp_, c, lo + h, h), tb_at(zq, yp_, c, lo + h, h), dn_y)
        send(yk(g), sb(g, 1), tb_at(zq, ym_, c, lo, n), tb_at(zq, ym_, c, lo, n), sib)
        send(yk(g), sb(g, 2), tb_at(zq, yp_, c, lo, n), tb_at(zq, yp_, c, lo, n), sib)

    def y_last(g):
        zq, lo, n = parcel(g)
        h, y2 = n // 2, (y + 2) % 4
        got(f"yf{g}", tb_at(zq, y2, c, lo, n))
        send(yk(g), sb(g, 3), tb_at(zq, y2, c, lo, n), tb_at(zq, y2, c, lo, n), sib)

    def sib_got(g, far=False):
        if g == 0:
            got_kb("sb0", 1024)
        else:
            got_kb(sb(g, 2 if far else 0), 128)

    def t_hop(h):
        for p in range(4):
            u, d = pl.ds(32 * p, 16), pl.ds(32 * p + 16, 16)
            if h == 1:
                src_u, src_d = tb.at[zh, y, c, u], tb.at[zh, y, c, d]
            else:
                src_u, src_d = ru.at[h - 2, p], rd.at[h - 2, p]
                got_kb(f"t{h - 1}{p}", 64)
            if h == 4:
                dst_u, dst_d = tb.at[((z + 5) % 8) // 4, y, c, u], tb.at[((z + 3) % 8) // 4, y, c, d]
            else:
                dst_u, dst_d = ru.at[h - 1, p], rd.at[h - 1, p]
            send("t", f"t{h}{p}", src_u, dst_u, up_z)
            send("t", f"t{h}{p}", src_d, dst_d, dn_z)

    def z_arrived(p):
        got(f"t4{p}", tb_at(1 - zh, y, c, 32 * p, 32))
        y_send(p + 1)

    line_send(1)
    x_send(0)
    t_hop(1)
    y_send(0)

    def pot_step(k, _):
        row = jnp.broadcast_to(pot_ref[pl.ds(k, 1), :], (128, 128))
        potb[k] = jnp.transpose(row)
        return 0

    lax.fori_loop(0, 16, pot_step, 0)

    def prep_rows(zq, yy):
        hi, lo = halves(jnp.transpose(tb[zq, yy].reshape(256, D)))
        cols = pl.ds(pl.multiple_of((zq * 4 + yy) * 256, 256), 256)
        tth[:, cols] = hi
        ttl[:, cols] = lo

    def split_x(k, _):
        rows = pl.ds(pl.multiple_of(k * 64, 64), 64)
        hi, lo = halves(xg[rows, :])
        xh[rows, :] = hi
        xl[rows, :] = lo
        return 0

    def plan_part(rows_t, pot, put):
        hi, lo = halves(rows_t)
        prod = dot(
            jnp.concatenate([hi, lo, hi], axis=1),
            jnp.concatenate([xh[...], xh[...], xl[...]], axis=0),
        )
        p = jnp.exp(prod[:, :F] * SCALE + jnp.concatenate([pot] * 4, axis=1))
        gd = prod[:, F:]
        put(p, gd)
        acc[0:8, :] += jnp.sum(p.reshape(32, 8, F), axis=0)
        acc[8:16, :] += jnp.sum((p * gd).reshape(32, 8, F), axis=0)

    def plan_block(zq, yy):
        def put(p, gd):
            pm[zq, yy] = p.reshape(2, TB, F)
            gdm[zq, yy] = gd.reshape(2, TB, F)

        pot = potb[pl.ds((zq * 4 + yy) * 2, 2)].reshape(256, 128)
        plan_part(tb[zq, yy].reshape(256, D), pot, put)

    def plan_piece(zq, two_y, p):
        rows = pl.ds(64 * p, 64)

        def put(p_, gd):
            for k, yy in enumerate(two_y):
                part = slice(128 * k, 128 * k + 128)
                pm[zq, yy, :, rows, :] = p_[part].reshape(2, 64, F)
                gdm[zq, yy, :, rows, :] = gd[part].reshape(2, 64, F)

        pot = jnp.concatenate([potb[pl.ds((zq * 4 + yy) * 2, 2), rows, :].reshape(128, 128) for yy in two_y], axis=0)
        tok = jnp.concatenate([tb[zq, yy, :, rows, :].reshape(128, D) for yy in two_y], axis=0)
        plan_part(tok, pot, put)

    def loop(n, step):
        lax.fori_loop(0, n, lambda k, _: (step(k), 0)[1], 0)

    acc[...] = jnp.zeros_like(acc)
    line_step(1)
    x_forward(0)
    t_hop(2)
    y_forward(0)
    line_step(2)
    by_step(1, x_forward)
    t_hop(3)
    y_last(0)
    line_step(3)
    by_step(2, x_forward)
    sib_got(0)
    t_hop(4)
    by_step(3, x_forward)
    loop(4, lambda k: prep_rows(zh, k))
    z_arrived(0)
    z_arrived(1)
    z_arrived(2)
    z_arrived(3)
    got_kb("xf", 512)
    lax.fori_loop(0, 8, split_x, 0)
    plan_block(zh, 0)
    y_forward(1)
    plan_block(zh, 1)
    y_forward(2)
    plan_block(zh, 2)
    y_forward(3)
    plan_block(zh, 3)
    y_forward(4)
    sib_got(1)
    sib_got(2)
    plan_piece(1 - zh, (y, ym_), 0)
    y_last(1)
    y_last(2)
    sib_got(3)
    sib_got(4)
    plan_piece(1 - zh, (y, ym_), 1)
    y_last(3)
    y_last(4)
    sib_got(1, True)
    sib_got(2, True)
    plan_piece(1 - zh, (yp_, (y + 2) % 4), 0)
    sib_got(3, True)
    sib_got(4, True)
    plan_piece(1 - zh, (yp_, (y + 2) % 4), 1)

    mine = st.at[t_me]
    mass_part = jnp.sum(acc[0:8, :], axis=0, keepdims=True)
    dots_part = jnp.sum(acc[8:16, :], axis=0, keepdims=True)
    for k in range(4):
        mine[k : k + 1, :] = mass_part[:, k * 128 : (k + 1) * 128]
        mine[k + 4 : k + 5, :] = dots_part[:, k * 128 : (k + 1) * 128]
    for k in range(1, 16):
        send("st", "st", mine, mine, text_peers[k - 1])

    loop(4, lambda k: prep_rows(1 - zh, k))

    def right_x(k, _):
        cols = pl.ds(pl.multiple_of(k * 128, 128), 128)
        hi, lo = halves(jnp.transpose(xg[:, cols]) * SCALE)
        rows = pl.ds(pl.multiple_of(F + k * 128, 128), 128)
        rh[rows, :] = hi
        rl[rows, :] = lo
        return 0

    def right_g(k, _):
        cols = pl.ds(pl.multiple_of(F + k * 128, 128), 128)
        hi, lo = halves(jnp.transpose(xg[:, cols]))
        rows = pl.ds(pl.multiple_of(k * 128, 128), 128)
        rh[rows, :] = hi
        rl[rows, :] = lo
        return 0

    lax.fori_loop(0, 4, right_x, 0)
    lax.fori_loop(0, 4, right_g, 0)

    got_kb("st", 60)
    total = jnp.sum(st[...], axis=0)
    mass = jnp.concatenate([total[k : k + 1, :] for k in range(4)], axis=1)
    inv = 1.0 / mass
    dots = jnp.concatenate([total[k : k + 1, :] for k in range(4, 8)], axis=1) / mass

    def weights(p, gd):
        sh = p * inv
        return halves(sh), halves(sh * (gd - dots))

    def right_product(sh, w):
        return dot(
            jnp.concatenate([sh[0], w[0], sh[1], w[1], sh[0], w[0]], axis=1),
            jnp.concatenate([rh[...], rh[...], rl[...]], axis=0),
        )

    def weigh(yy):
        _, w = weights(pm[zh, yy].reshape(256, F), gdm[zh, yy].reshape(256, F))
        wh[zh, yy] = w[0].reshape(2, TB, F)
        wl[zh, yy] = w[1].reshape(2, TB, F)

    def text_block(d):
        yd = (y + d) % 4
        sh = halves(pm[zh, yd].reshape(256, F) * inv)
        out = right_product(sh, (wh[zh, yd].reshape(256, F), wl[zh, yd].reshape(256, F)))
        cp[zh, yd] = out.reshape(2, TB, D)
        send("c", f"cs{d}", cp.at[zh, yd, 1 - c], sbuf.at[0, d], sib)

    def chip_sum(d):
        got(f"cs{d}", sbuf.at[0, d])
        return cp[zh, (y + d) % 4, c] + sbuf[0, d]

    def piece(p):
        return pl.ds(32 * p, 32)

    def text_piece(p):
        zq, rows = 1 - zh, piece(p)
        sh, w = weights(pm[zq, :, :, rows, :].reshape(256, F), gdm[zq, :, :, rows, :].reshape(256, F))
        wh[zq, :, :, rows, :] = w[0].reshape(4, 2, 32, F)
        wl[zq, :, :, rows, :] = w[1].reshape(4, 2, 32, F)
        cp[zq, :, :, rows, :] = right_product(sh, w).reshape(4, 2, 32, D)
        send("c", f"ct{p}", cp.at[zq, :, 1 - c, rows], sbuf.at[1, :, rows], sib)

    def straight(p):
        rows = piece(p)
        got(f"ct{p}", sbuf.at[1, :, rows])
        ys[1, :, rows] = cp[1 - zh, :, c, rows] + sbuf[1, :, rows]
        y2 = (y + 2) % 4
        for n in (0, 1) if p == 0 else (p + 1,):
            rows = pl.ds(*PARTS[n])
            send("q", f"q{n}", ys.at[1, y2, rows], qfar.at[rows], dev(zh, y2, c, zl, x))
            send("q", f"q{n}", ys.at[1, yp_, rows], ry1.at[1, 0, rows], up_y)
            send("q", f"q{n}", ys.at[1, ym_, rows], ry1.at[1, 1, rows], dn_y)

    def own_z(n):
        rows = pl.ds(*PARTS[n])
        got_kb(f"q{n}", 6 * PARTS[n][1])
        ys[1, y, rows] += qfar[rows] + (ry1[1, 0, rows] + ry1[1, 1, rows])
        send("q", "w", ys.at[1, y, rows], zr.at[rows], far_z)

    def upper(p):
        return pl.ds(64 * p, 32)

    def lower(p):
        return pl.ds(64 * p + 32, 32)

    def far_y():
        ys[0, 2] = chip_sum(2)
        for p in range(2):
            send("r", f"ra{p}", ys.at[0, 2, upper(p)], ry2.at[p, 0], up_y)
            send("r", f"ra{p}", ys.at[0, 2, lower(p)], ry2.at[p, 1], dn_y)

    def free_y():
        ys[0, 1] = chip_sum(1)
        ys[0, 3] = chip_sum(3)
        for p in range(2):
            send("r", f"rb{p}", ys.at[0, 1, lower(p)], ry1.at[0, 0, lower(p)], up_y)
            send("r", f"rb{p}", ys.at[0, 3, upper(p)], ry1.at[0, 1, upper(p)], dn_y)

    def near_y(p):
        got_kb(f"ra{p}", 128)
        ys[0, 1, upper(p)] += ry2[p, 0]
        send("r", f"rb{p}", ys.at[0, 1, upper(p)], ry1.at[0, 0, upper(p)], up_y)
        ys[0, 3, lower(p)] += ry2[p, 1]
        send("r", f"rb{p}", ys.at[0, 3, lower(p)], ry1.at[0, 1, lower(p)], dn_y)

    def own_y(p):
        got_kb(f"rb{p}", 256)
        rows = pl.ds(64 * p, 64)
        ys[0, 0, rows] += ry1[0, 0, rows] + ry1[0, 1, rows]

    def speech_rows(m):
        rows = pl.ds(m * 256, 256)
        hi, lo = tth[rows, :], ttl[rows, :]
        out = dot(
            jnp.concatenate([hi, lo, hi], axis=1),
            jnp.concatenate([wh[...].reshape(T, F), wh[...].reshape(T, F), wl[...].reshape(T, F)], axis=0),
        )
        sp[pl.ds(m * 2, 2)] = out.reshape(2, 4, 32, F)

    x2 = (x + 2) % 4
    top, low = pl.ds(0, 16), pl.ds(16, 16)

    def far_x(m):
        two = pl.ds(2 * m, 2)
        send("u", f"ua{m}", sp.at[two, x2, top], rx2.at[0, two], up_x)
        send("u", f"ua{m}", sp.at[two, x2, low], rx2.at[1, two], dn_x)
        send("u", f"ub{m}", sp.at[two, xp_, low], rx1.at[0, two, low], up_x)
        send("u", f"ub{m}", sp.at[two, xm_, top], rx1.at[1, two, top], dn_x)

    def near_x(m):
        two = pl.ds(2 * m, 2)
        got_kb(f"ua{m}", 128)
        xs[0, two] = sp[two, xp_, 0:16] + rx2[0, two]
        send("u", f"ub{m}", xs.at[0, two], rx1.at[0, two, top], up_x)
        xs[1, two] = sp[two, xm_, 16:32] + rx2[1, two]
        send("u", f"ub{m}", xs.at[1, two], rx1.at[1, two, low], dn_x)

    def own_x(m):
        two = pl.ds(2 * m, 2)
        got_kb(f"ub{m}", 256)
        xo[two] = sp[two, x] + (rx1[0, two] + rx1[1, two])

    text_piece(0)
    text_piece(1)
    straight(0)
    text_piece(2)
    straight(1)
    text_piece(3)
    straight(2)
    loop(4, weigh)
    straight(3)
    own_z(0)
    speech_rows(0)
    far_x(0)
    own_z(1)
    speech_rows(1)
    far_x(1)
    text_block(2)
    own_z(2)
    text_block(1)
    far_y()
    near_x(0)
    text_block(3)
    own_z(3)
    near_x(1)
    text_block(0)
    free_y()
    own_z(4)
    own_x(0)
    own_x(1)
    for k, zt in enumerate((3 - zl, (zl + 2) % 4, zl + 1 - 2 * (zl % 2))):
        send("v", "v", xo.at[zt], rz.at[k], dev(zh, y, c, zt, x))
    ys[0, 0] = chip_sum(0)
    near_y(0)
    near_y(1)
    own_y(0)
    own_y(1)
    got("w", zr)
    tg_ref[...] = ys[0, 0] + zr[...]
    got("v", rz)
    sg_ref[...] = (xo[zl] + (rz[0] + (rz[1] + rz[2]))) * SCALE
    for j in (1, 2, 3):
        for fits, one in (line_up(j), line_down(j)):

            @pl.when(fits)
            def _(one=one):
                one.wait_send()

    for r in (1, 3):
        sent["x"] += 2 * 32 * 4096 + 2 * 16 * 4096
    for kind, size in sent.items():
        if size:
            copy(kind, "x0", bulk(size), bulk(size), sib).wait_send()


def finish(sg_ref, tg_ref, sg_out, tg_out):
    sg_out[...] = sg_ref[...]
    tg_out[...] = tg_ref[...]


def solution(mesh):
    def v(shape, kind=F32):
        return pltpu.VMEM(shape, kind)

    scratch = [
        v((D, 2 * F)), v((2, 4, 2, TB, D)), v((D, 2 * F), BF), v((D, 2 * F), BF),
        v((D, T), BF), v((D, T), BF), v((2 * F, D), BF), v((2 * F, D), BF),
        v((16, TB, 128)), v((2, 4, 2, TB, F)), v((2, 4, 2, TB, F)), v((2, 4, 2, TB, F), BF), v((2, 4, 2, TB, F), BF), v((16, F)), v((16, 8, 128)),
        v((2, 4, 2, TB, D)), v((2, 4, TB, D)), v((2, 4, TB, D)), v((2, 2, 32, D)), v((2, 2, TB, D)), v((TB, D)),
        v((TB, D)), v((3, 4, 16, D)), v((3, 4, 16, D)),
        v((4, 4, 32, F)), v((2, 4, 16, F)), v((4, 32, F)), v((2, 4, 16, F)), v((2, 4, 32, F)), v((3, 32, F)),
        pltpu.SemaphoreType.DMA((len(KINDS),)),
        pltpu.SemaphoreType.DMA((len(GROUPS),)),
        pltpu.SemaphoreType.DMA((3,)),
    ]
    anywhere = pl.BlockSpec(memory_space=pl.ANY)
    vmem = pl.BlockSpec(memory_space=pltpu.VMEM)
    call = pl.pallas_call(
        kernel,
        out_shape=(jax.ShapeDtypeStruct((32, F), F32), jax.ShapeDtypeStruct((TB, D), F32)),
        in_specs=[anywhere, anywhere, anywhere, vmem],
        out_specs=(vmem, vmem),
        scratch_shapes=scratch,
        compiler_params=pltpu.CompilerParams(
            collective_id=0, has_side_effects=True, vmem_limit_bytes=62 * 1024 * 1024
        ),
    )

    last = pl.pallas_call(
        finish,
        out_shape=(jax.ShapeDtypeStruct((32, F), F32), jax.ShapeDtypeStruct((TB, D), F32)),
        in_specs=[vmem, vmem],
        out_specs=(vmem, vmem),
    )

    def shards(speech_feat, text_feat, text_pot, map_grad):
        sg, tg = last(*call(speech_feat.T, map_grad.T, text_feat, text_pot.reshape(16, 128)))
        return sg.T, tg

    return jax.shard_map(
        shards,
        mesh=mesh,
        in_specs=(P("speech", "text"), P(("text", "speech"), None), P("text"), P("speech", "text")),
        out_specs=(P("speech", "text"), P(("text", "speech"), None)),
        check_vma=False,
    )
```
